32 devices in a mesh: seq: 32 (over z, y, x, core).
Axes of the slice: x: 2, y: 2, z: 4, core: 2. Of those that a mesh axis runs over, the one named last changes fastest.
Arguments:
- block_input: float32 [4096, 1024], P('seq'), may hold values from -6 to 6
- cotangent: float32 [4096, 1024], P('seq'), may hold values from -6 to 6
- attn_gain: bfloat16 [1024], P('seq'), may hold values from 0.5 to 1.5
- w_query: bfloat16 [1024, 512], P('seq'), may hold values from -0.1875 to 0.1875
- w_key: bfloat16 [1024, 512], P('seq'), may hold values from -0.1875 to 0.1875
- w_value: bfloat16 [1024, 1024], P('seq'), may hold values from -0.1875 to 0.1875
- w_outgate: bfloat16 [1024, 1024], P('seq'), may hold values from -0.1875 to 0.1875
- w_decay_down: bfloat16 [1024, 16], P('seq'), may hold values from -0.1875 to 0.1875
- w_decay_up: bfloat16 [16, 512], P(None, 'seq'), may hold values from -2.5 to 2.5
- decay_bias: bfloat16 [512], P('seq')
- head_gain: bfloat16 [256], P('seq'), may hold values from 0.5 to 1.5
- w_out: bfloat16 [1024, 1024], P('seq'), may hold values from -0.1875 to 0.1875
- mlp_gain: bfloat16 [1024], P('seq'), may hold values from 0.5 to 1.5
- w_gate: bfloat16 [1024, 2816], P('seq'), may hold values from -0.1875 to 0.1875
- w_up: bfloat16 [1024, 2816], P('seq'), may hold values from -0.1875 to 0.1875
- w_down: bfloat16 [2816, 1024], P('seq'), may hold values from -0.109375 to 0.109375
Outputs:
- block_output: float32 [4096, 1024], P('seq')
- input_grad: float32 [4096, 1024], P('seq')
- grad_attn_gain: float32 [1024], P('seq')
- grad_query: float32 [1024, 512], P('seq')
- grad_key: float32 [1024, 512], P('seq')
- grad_value: float32 [1024, 1024], P('seq')
- grad_outgate: float32 [1024, 1024], P('seq')
- grad_decay_down: float32 [1024, 16], P('seq')
- grad_decay_up: float32 [16, 512], P(None, 'seq')
- grad_decay_bias: float32 [512], P('seq')
- grad_head_gain: float32 [256], P('seq')
- grad_out: float32 [1024, 1024], P('seq')
- grad_mlp_gain: float32 [1024], P('seq')
- grad_gate: float32 [1024, 2816], P('seq')
- grad_up: float32 [1024, 2816], P('seq')
- grad_down: float32 [2816, 1024], P('seq')
The draws below stay inside these ranges and needn't reach their ends.
All inputs are finite; a program needn't handle non-finite values.
Results may differ from the reference program's by a relative error of at most 0.02.
Values may be sent and summed in bfloat16 or wider, within the bound.
No kernel may reach another device: no remote copies, remote signals or barrier semaphores. Data moves between devices by JAX's collectives and lax.ppermute only.
A program may use at most 320 MiB of HBM per device.

```python
import jax
import jax.numpy as jnp
from jax import lax

D = 1024
H = 4
DK = 128
VALUE_WIDTH = 256
R = 16
FF = 2816
GROUP = 64
TOKENS = 4096
KD = 512
VD = 1024


def draw_decay_bias(key, part):
    choose_key, slow_key, fast_key = jax.random.split(key, 3)
    choose = jax.random.randint(choose_key, (KD,), 0, 2)
    slow_mask = choose > 0
    spread = jax.random.uniform(slow_key, (KD,), jnp.float32, 0.3, 2.0)
    slow_bias = jnp.log(TOKENS / (16.0 * spread)) + 1.3
    fast_bias = jax.random.uniform(fast_key, (KD,), jnp.float32, 1.0, 2.0)
    return jnp.where(slow_mask, slow_bias, fast_bias).astype(jnp.bfloat16)


def block_levels(key, extent, pieces, smallest, high):
    def one(position, shards_of):
        draws = jax.random.uniform(jax.random.fold_in(jax.random.fold_in(key, 6), position), (shards_of,), jnp.float32, smallest / len(pieces), high / len(pieces))
        return jnp.repeat(jnp.exp(draws), extent[position] // shards_of).reshape((-1,) + (1,) * (len(extent) - position - 1))

    level = one(*pieces[0])
    for cut in pieces[1:]:
        level = level * one(*cut)
    return level


def normal_values(stream_key, dims, width, reach, cuts=(), held_as=jnp.bfloat16):
    entries = width * jax.random.normal(stream_key, dims, jnp.float32)
    if cuts:
        entries = entries * block_levels(stream_key, dims, cuts, -0.22, 0.18)
    return jnp.clip(entries, -reach, reach).astype(held_as)


def setup_inputs(seed: int = 0) -> dict:
    splits = jax.random.split(jax.random.key(seed), 17)
    block_input = normal_values(splits[0], (TOKENS, D), 1.0, 6.0, ((0, 32),), jnp.float32)
    cotangent = normal_values(splits[1], (TOKENS, D), 1.0, 6.0, ((0, 32),), jnp.float32)
    attn_gain = jnp.clip(1.0 + 0.1 * jax.random.normal(splits[2], (D,), jnp.float32), 0.5, 1.5).astype(jnp.bfloat16)
    w_query = normal_values(splits[3], (D, KD), D ** -0.5, 0.1875, ((0, 32),))
    w_key = normal_values(splits[4], (D, KD), D ** -0.5, 0.1875, ((0, 32),))
    w_value = normal_values(splits[5], (D, VD), D ** -0.5, 0.1875, ((0, 32),))
    w_outgate = normal_values(splits[6], (D, VD), D ** -0.5, 0.1875, ((0, 32),))
    w_decay_down = normal_values(splits[7], (D, R), D ** -0.5, 0.1875, ((0, 32),))
    w_decay_up = normal_values(splits[8], (R, KD), 0.4, 2.5, ((1, 32),))
    decay_bias = draw_decay_bias(jax.random.fold_in(splits[16], 71), 0)
    head_gain = jnp.clip(1.0 + 0.1 * jax.random.normal(splits[10], (VALUE_WIDTH,), jnp.float32), 0.5, 1.5).astype(jnp.bfloat16)
    w_out = normal_values(splits[11], (VD, D), VD ** -0.5, 0.1875, ((0, 32),))
    mlp_gain = jnp.clip(1.0 + 0.1 * jax.random.normal(splits[12], (D,), jnp.float32), 0.5, 1.5).astype(jnp.bfloat16)
    w_gate = normal_values(splits[13], (D, FF), D ** -0.5, 0.1875, ((0, 32),))
    w_up = normal_values(splits[14], (D, FF), D ** -0.5, 0.1875, ((0, 32),))
    w_down = normal_values(splits[15], (FF, D), FF ** -0.5, 0.109375, ((0, 32),))
    return dict(block_input=block_input, cotangent=cotangent, attn_gain=attn_gain, w_query=w_query, w_key=w_key, w_value=w_value, w_outgate=w_outgate, w_decay_down=w_decay_down, w_decay_up=w_decay_up, decay_bias=decay_bias, head_gain=head_gain, w_out=w_out, mlp_gain=mlp_gain, w_gate=w_gate, w_up=w_up, w_down=w_down)


EPS = 1e-05
GATE_NORM = 16.0
TOP_PRECISION = lax.Precision.HIGHEST

def matmul(left_side, right_side):
    return jnp.dot(left_side, right_side, preferred_element_type=jnp.float32)

def times_back(left_side, right_side):
    return lax.dot_general(left_side, right_side, (((1,), (1,)), ((), ())), preferred_element_type=jnp.float32)

def outer_sum(left_side, right_side):
    return lax.dot_general(left_side, right_side, (((0,), (0,)), ((), ())), preferred_element_type=jnp.float32)

def rms_norm(matrix, gain):
    scaling = lax.rsqrt(lax.optimization_barrier(jnp.mean(matrix * matrix, axis=-1, keepdims=True)) + EPS)
    return matrix * scaling * gain

def swiglu(gate_pre, up_pre):
    return jax.nn.silu(gate_pre) * up_pre

def split_into_heads(matrix, columns):
    return matrix.reshape(matrix.shape[0] // GROUP, GROUP, H, columns).transpose(2, 0, 1, 3)

def from_heads(blocks):
    return blocks.transpose(1, 2, 0, 3).reshape(blocks.shape[1] * blocks.shape[2], blocks.shape[0] * blocks.shape[3])

def to_front(tensor):
    return jnp.moveaxis(tensor, 1, 0)

def group_pass(query_blocks, key_blocks, value_blocks, decay_blocks, initial):
    inner = jnp.cumsum(decay_blocks, axis=2)
    ending = inner[:, :, -1:, :]
    query_in = query_blocks * jnp.exp(inner)
    key_in = key_blocks * jnp.exp(-inner)
    key_end = key_blocks * jnp.exp(ending - inner)
    length = query_blocks.shape[2]
    causal = jnp.tril(jnp.ones((length, length), jnp.float32))
    scores = jnp.einsum('hnck,hnsk->hncs', query_in, key_in, precision=TOP_PRECISION) * causal
    within = jnp.einsum('hncs,hnsv->hncv', scores, value_blocks, precision=TOP_PRECISION)

    def advance(carried_state, sequence_segments):
        query_segment, key_segment, value_segment, fading_factor = sequence_segments
        block_result = jnp.einsum('waq,wqo->wao', query_segment, carried_state, precision=TOP_PRECISION)
        carried_state = fading_factor[:, 0, :, None] * carried_state + jnp.einsum('fjb,fjq->fbq', key_segment, value_segment, precision=TOP_PRECISION)
        return (carried_state, block_result)
    final, across_pieces = lax.scan(advance, initial, (to_front(query_in), to_front(key_end), to_front(value_blocks), to_front(jnp.exp(ending))))
    return (within + to_front(across_pieces), final)

def post_gate(mixer, outgate, head_gain):
    tokens_here = mixer.shape[0]
    per_head = mixer.reshape(tokens_here, H, VALUE_WIDTH)
    normed = rms_norm(per_head, head_gain).reshape(tokens_here, H * VALUE_WIDTH)
    return normed * outgate * jax.nn.sigmoid(outgate)

def mixer_piece(query, keys, values, outgate, decay_logit, head_gain):
    log_decay = jax.nn.log_sigmoid(decay_logit) / GATE_NORM
    zero_state = jnp.zeros((H, DK, VALUE_WIDTH), jnp.float32)
    blocks, final = group_pass(split_into_heads(query, DK), split_into_heads(keys, DK), split_into_heads(values, VALUE_WIDTH), split_into_heads(log_decay, DK), zero_state)
    return post_gate(from_heads(blocks), outgate, head_gain)

def reference(block_input, cotangent, attn_gain, w_query, w_key, w_value, w_outgate, w_decay_down, w_decay_up, decay_bias, head_gain, w_out, mlp_gain, w_gate, w_up, w_down):
    scaling = DK ** (-0.5)
    normed, norm_back = jax.vjp(rms_norm, block_input, attn_gain.astype(jnp.float32))
    normed_in = normed.astype(jnp.bfloat16)
    query = matmul(normed_in, w_query) * scaling
    keys = matmul(normed_in, w_key)
    values = matmul(normed_in, w_value)
    outgate = matmul(normed_in, w_outgate)
    low_rank = matmul(normed_in, w_decay_down).astype(jnp.bfloat16)
    decay_logit = matmul(low_rank, w_decay_up) + decay_bias.astype(jnp.float32)
    gated_full, mixer_back = jax.vjp(mixer_piece, query, keys, values, outgate, decay_logit, head_gain.astype(jnp.float32))
    gated = gated_full.astype(jnp.bfloat16)
    hidden_state = block_input + matmul(gated, w_out)
    mlp_full, mlp_back = jax.vjp(rms_norm, hidden_state, mlp_gain.astype(jnp.float32))
    mlp_normed = mlp_full.astype(jnp.bfloat16)
    gate_pre = matmul(mlp_normed, w_gate)
    up_pre = matmul(mlp_normed, w_up)
    activ_full, activ_back = jax.vjp(swiglu, gate_pre, up_pre)
    activ = activ_full.astype(jnp.bfloat16)
    block_output = hidden_state + matmul(activ, w_down)
    cot_in = cotangent.astype(jnp.bfloat16)
    grad_down = outer_sum(activ, cot_in)
    d_activ = times_back(cot_in, w_down)
    d_gate_full, d_up_full = activ_back(d_activ)
    d_gate = d_gate_full.astype(jnp.bfloat16)
    d_up = d_up_full.astype(jnp.bfloat16)
    grad_gate = outer_sum(mlp_normed, d_gate)
    grad_up = outer_sum(mlp_normed, d_up)
    d_mlp_normed = times_back(d_gate, w_gate) + times_back(d_up, w_up)
    d_hidden_norm, grad_mlp_gain = mlp_back(d_mlp_normed)
    d_hidden = cotangent + d_hidden_norm
    d_hidden_in = d_hidden.astype(jnp.bfloat16)
    grad_out = outer_sum(gated, d_hidden_in)
    d_gated = times_back(d_hidden_in, w_out)
    d_query, d_keys, d_values, d_outgate, d_logit, grad_head_gain = mixer_back(d_gated)
    grad_decay_bias = lax.optimization_barrier(jnp.sum(d_logit, axis=0))
    d_logit_in = d_logit.astype(jnp.bfloat16)
    grad_decay_up = outer_sum(low_rank, d_logit_in)
    d_low = times_back(d_logit_in, w_decay_up).astype(jnp.bfloat16)
    grad_decay_down = outer_sum(normed_in, d_low)
    d_query_in = (d_query * scaling).astype(jnp.bfloat16)
    d_keys_in = d_keys.astype(jnp.bfloat16)
    d_values_in = d_values.astype(jnp.bfloat16)
    d_outgate_in = d_outgate.astype(jnp.bfloat16)
    grad_query = outer_sum(normed_in, d_query_in)
    grad_key = outer_sum(normed_in, d_keys_in)
    grad_value = outer_sum(normed_in, d_values_in)
    grad_outgate = outer_sum(normed_in, d_outgate_in)
    d_normed = times_back(d_query_in, w_query) + times_back(d_keys_in, w_key) + times_back(d_values_in, w_value)
    d_normed = d_normed + times_back(d_outgate_in, w_outgate) + times_back(d_low, w_decay_down)
    d_input_norm, grad_attn_gain = norm_back(d_normed)
    input_grad = d_hidden + d_input_norm
    return (block_output, input_grad, grad_attn_gain, grad_query, grad_key, grad_value, grad_outgate, grad_decay_down, grad_decay_up, grad_decay_bias, grad_head_gain, grad_out, grad_mlp_gain, grad_gate, grad_up, grad_down)
```

```python
import jax
import jax.numpy as jnp
from jax import lax
from jax.sharding import PartitionSpec as P

H = 4
DK = 128
VALUE_WIDTH = 256
GROUP = 64


EPS = 1e-05
GATE_NORM = 16.0
TOP_PRECISION = lax.Precision.HIGHEST


LANES = 128


def pack_small(pieces, rows):
    flat = jnp.concatenate([piece.reshape(-1) for piece in pieces])
    return jnp.pad(flat, (0, rows * LANES - flat.shape[0])).reshape(rows, LANES)


def pack_small_sums(pieces, devices, rows):
    flat = jnp.concatenate([piece.reshape(devices, -1) for piece in pieces], axis=1)
    flat = jnp.pad(flat, ((0, 0), (0, rows * LANES - flat.shape[1])))
    return flat.reshape(devices * rows, LANES)


def unpack_small(flat, shapes):
    pieces, at = [], 0
    for shape in shapes:
        size = 1
        for extent in shape:
            size *= extent
        pieces.append(flat[..., at : at + size].reshape(flat.shape[:-1] + shape))
        at += size
    return pieces


def column_slices(array, widths):
    pieces, at = [], 0
    for width in widths:
        pieces.append(array[:, at : at + width])
        at += width
    return pieces


def three_pieces(value):
    high = value.astype(jnp.bfloat16)
    rest = value - high.astype(jnp.float32)
    middle = rest.astype(jnp.bfloat16)
    low = (rest - middle.astype(jnp.float32)).astype(jnp.bfloat16)
    return jnp.stack([high, middle, low])


def between(log_fading, mine, forward):
    count = log_fading.shape[0]
    j = lax.broadcasted_iota(jnp.int32, (count, count), 0)
    k = lax.broadcasted_iota(jnp.int32, (count, count), 1)
    if forward:
        inside = (j < k) & (k < mine)
        taken = jnp.arange(count) < mine
    else:
        inside = (k < j) & (k > mine)
        taken = jnp.arange(count) > mine
    span = jnp.dot(inside.astype(jnp.float32), log_fading, precision=TOP_PRECISION)
    return jnp.where(taken[:, None], jnp.exp(span), 0.0)


def matmul(left_side, right_side):
    return jnp.dot(left_side, right_side, preferred_element_type=jnp.float32)


def times_back(left_side, right_side):
    return lax.dot_general(
        left_side, right_side, (((1,), (1,)), ((), ())), preferred_element_type=jnp.float32
    )


def outer_sum(left_side, right_side):
    return lax.dot_general(
        left_side, right_side, (((0,), (0,)), ((), ())), preferred_element_type=jnp.float32
    )


def rms_norm(matrix, gain):
    scaling = lax.rsqrt(jnp.mean(matrix * matrix, axis=-1, keepdims=True) + EPS)
    return matrix * scaling * gain


def swiglu(gate_pre, up_pre):
    return jax.nn.silu(gate_pre) * up_pre


def split_into_heads(matrix, columns):
    return matrix.reshape(matrix.shape[0] // GROUP, GROUP, H, columns).transpose(2, 0, 1, 3)


def from_heads(blocks):
    return blocks.transpose(1, 2, 0, 3).reshape(
        blocks.shape[1] * blocks.shape[2], blocks.shape[0] * blocks.shape[3]
    )


def to_front(tensor):
    return jnp.moveaxis(tensor, 1, 0)


def group_pass(query_blocks, key_blocks, value_blocks, decay_blocks, initial):
    inner = jnp.cumsum(decay_blocks, axis=2)
    ending = inner[:, :, -1:, :]
    query_in = query_blocks * jnp.exp(inner)
    key_in = key_blocks * jnp.exp(-inner)
    key_end = key_blocks * jnp.exp(ending - inner)
    length = query_blocks.shape[2]
    causal = jnp.tril(jnp.ones((length, length), jnp.float32))
    scores = jnp.einsum("hnck,hnsk->hncs", query_in, key_in, precision=TOP_PRECISION) * causal
    within = jnp.einsum("hncs,hnsv->hncv", scores, value_blocks, precision=TOP_PRECISION)

    def advance(carried_state, sequence_segments):
        query_segment, key_segment, value_segment, fading_factor = sequence_segments
        block_result = jnp.einsum(
            "waq,wqo->wao", query_segment, carried_state, precision=TOP_PRECISION
        )
        carried_state = fading_factor[:, 0, :, None] * carried_state + jnp.einsum(
            "fjb,fjq->fbq", key_segment, value_segment, precision=TOP_PRECISION
        )
        return (carried_state, block_result)

    final, across_pieces = lax.scan(
        advance,
        initial,
        (to_front(query_in), to_front(key_end), to_front(value_blocks), to_front(jnp.exp(ending))),
    )
    return (within + to_front(across_pieces), final)


def post_gate(mixer, outgate, head_gain):
    tokens_here = mixer.shape[0]
    per_head = mixer.reshape(tokens_here, H, VALUE_WIDTH)
    normed = rms_norm(per_head, head_gain).reshape(tokens_here, H * VALUE_WIDTH)
    return normed * outgate * jax.nn.sigmoid(outgate)


def local_pass(query, keys, values, decay_logit):
    log_decay = jax.nn.log_sigmoid(decay_logit) / GATE_NORM
    query_blocks = split_into_heads(query, DK)
    decay_blocks = split_into_heads(log_decay, DK)
    zero_state = jnp.zeros((H, DK, VALUE_WIDTH), jnp.float32)
    local_out, local_state = group_pass(
        query_blocks,
        split_into_heads(keys, DK),
        split_into_heads(values, VALUE_WIDTH),
        decay_blocks,
        zero_state,
    )
    layout = decay_blocks.shape
    cumulative = jnp.cumsum(
        decay_blocks.reshape(layout[0], layout[1] * layout[2], layout[3]), axis=1
    ).reshape(layout)
    log_fading = cumulative[:, -1, -1, :]
    query_fading = query_blocks * jnp.exp(cumulative)
    return (query_fading, log_fading, local_out, local_state)


def finish(sequence_segments, incoming_state):
    query_fading, log_fading, local_out, local_state = sequence_segments
    across_pieces = jnp.einsum(
        "qwxg,qgf->qwxf", query_fading, incoming_state, precision=TOP_PRECISION
    )
    return (
        from_heads(local_out + across_pieces),
        jnp.exp(log_fading)[:, :, None] * incoming_state + local_state,
    )


def local(
    block_input,
    cotangent,
    attn_gain,
    w_query,
    w_key,
    w_value,
    w_outgate,
    w_decay_down,
    w_decay_up,
    decay_bias,
    head_gain,
    w_out,
    mlp_gain,
    w_gate,
    w_up,
    w_down,
):
    count, mine = (lax.axis_size("seq"), lax.axis_index("seq"))
    rows = w_query.shape[0]
    key_width, value_width, rank = (w_query.shape[1], w_value.shape[1], w_decay_down.shape[1])
    hidden = w_gate.shape[1]
    small_shapes = (w_decay_up.shape, attn_gain.shape, mlp_gain.shape, decay_bias.shape, head_gain.shape)
    first = jnp.concatenate(
        [
            w_query,
            w_key,
            w_value,
            w_outgate,
            jnp.pad(w_decay_down, ((0, 0), (0, LANES - rank))),
            pack_small((w_decay_up, attn_gain, mlp_gain, decay_bias, head_gain), rows),
        ],
        axis=1,
    )
    first = lax.all_gather(first, "seq", axis=0, tiled=True)
    second = jnp.concatenate([w_out, w_gate, w_up], axis=1)
    second = lax.all_gather(second, "seq", axis=0, tiled=True)
    down_full = lax.all_gather(w_down, "seq", axis=0, tiled=True)
    widths = (key_width, key_width, value_width, value_width)
    wide = 2 * key_width + 2 * value_width
    projection = first[:, : wide + LANES]
    small = first[:, wide + LANES :].reshape(count, rows * LANES)
    up_pieces, attn_full, mlp_full_gain, bias_full, head_full = unpack_small(small, small_shapes)
    decay_up_full = up_pieces.transpose(1, 0, 2).reshape(rank, key_width)
    attn_full, mlp_full_gain, bias_full, head_full = (
        piece.reshape(-1).astype(jnp.float32) for piece in (attn_full, mlp_full_gain, bias_full, head_full)
    )
    out_full = second[:, : w_out.shape[1]]
    gate_up = second[:, w_out.shape[1] :]
    scaling = DK ** (-0.5)
    normed, norm_back = jax.vjp(rms_norm, block_input, attn_full)
    normed_in = normed.astype(jnp.bfloat16)
    query, keys, values, outgate, low_rank = column_slices(
        matmul(normed_in, projection), widths + (rank,)
    )
    query = query * scaling
    low_rank = low_rank.astype(jnp.bfloat16)
    decay_logit = matmul(low_rank, decay_up_full) + bias_full
    sequence_segments, local_back = jax.vjp(local_pass, query, keys, values, decay_logit)
    state = sequence_segments[3].reshape(key_width, VALUE_WIDTH).astype(jnp.bfloat16)
    log_rows = three_pieces(sequence_segments[1].reshape(-1)).reshape(-1, VALUE_WIDTH)
    extra = log_rows.shape[0]
    log_rows = jnp.pad(log_rows, ((0, -extra % 16), (0, 0)))
    everything = lax.all_gather(jnp.concatenate([state, log_rows], axis=0), "seq")
    log_fading = everything[:, key_width : key_width + extra].astype(jnp.float32)
    log_fading = log_fading.reshape(count, 3, key_width).sum(axis=1)
    weight = between(log_fading, mine, True)
    incoming_state = jnp.sum(
        weight[:, :, None] * everything[:, :key_width].astype(jnp.float32), axis=0
    ).reshape(H, DK, VALUE_WIDTH)
    mixer, state_after = finish(sequence_segments, incoming_state)
    gated_full, post_back = jax.vjp(post_gate, mixer, outgate, head_full)
    gated = gated_full.astype(jnp.bfloat16)
    hidden_state = block_input + matmul(gated, out_full)
    mlp_full, mlp_back = jax.vjp(rms_norm, hidden_state, mlp_full_gain)
    mlp_normed = mlp_full.astype(jnp.bfloat16)
    gate_pre, up_pre = column_slices(matmul(mlp_normed, gate_up), (hidden, hidden))
    activ_full, activ_back = jax.vjp(swiglu, gate_pre, up_pre)
    activ = activ_full.astype(jnp.bfloat16)
    block_output = hidden_state + matmul(activ, down_full)
    cot_in = cotangent.astype(jnp.bfloat16)
    grad_down = outer_sum(activ, cot_in)
    d_activ = times_back(cot_in, down_full)
    d_gate_full, d_up_full = activ_back(d_activ)
    d_gate = d_gate_full.astype(jnp.bfloat16)
    d_up = d_up_full.astype(jnp.bfloat16)
    d_gate_up = jnp.concatenate([d_gate, d_up], axis=1)
    grad_gate_up = outer_sum(mlp_normed, d_gate_up)
    d_mlp_normed = times_back(d_gate_up, gate_up)
    d_hidden_norm, grad_mlp_gain = mlp_back(d_mlp_normed)
    d_hidden = cotangent + d_hidden_norm
    d_hidden_in = d_hidden.astype(jnp.bfloat16)
    grad_out = outer_sum(gated, d_hidden_in)
    d_gated = times_back(d_hidden_in, out_full)
    mixer_gradient, d_outgate, grad_head_gain = post_back(d_gated)
    state_gradient = jnp.einsum(
        "ryfm,ryfj->rmj",
        sequence_segments[0],
        split_into_heads(mixer_gradient, VALUE_WIDTH),
        precision=TOP_PRECISION,
    )
    everything_back = lax.all_gather(
        state_gradient.reshape(key_width, VALUE_WIDTH).astype(jnp.bfloat16), "seq"
    )
    weight_back = between(log_fading, mine, False)
    after = jnp.sum(weight_back[:, :, None] * everything_back.astype(jnp.float32), axis=0)
    after = after.reshape(H, DK, VALUE_WIDTH)
    finish_value, finish_back = jax.vjp(finish, sequence_segments, incoming_state)
    d_pieces, d_incoming = finish_back((mixer_gradient, after))
    d_query, d_keys, d_values, d_logit = local_back(d_pieces)
    grad_decay_bias = jnp.sum(d_logit, axis=0)
    d_logit_in = d_logit.astype(jnp.bfloat16)
    grad_decay_up = outer_sum(low_rank, d_logit_in)
    d_low = times_back(d_logit_in, decay_up_full).astype(jnp.bfloat16)
    d_first = jnp.concatenate(
        [
            (d_query * scaling).astype(jnp.bfloat16),
            d_keys.astype(jnp.bfloat16),
            d_values.astype(jnp.bfloat16),
            d_outgate.astype(jnp.bfloat16),
            jnp.pad(d_low, ((0, 0), (0, LANES - rank))),
        ],
        axis=1,
    )
    grad_first = outer_sum(normed_in, d_first)
    d_normed = times_back(d_first, projection)
    d_input_norm, grad_attn_gain = norm_back(d_normed)
    input_grad = d_hidden + d_input_norm

    def scattered(partial):
        return lax.psum_scatter(
            partial.astype(jnp.bfloat16), "seq", scatter_dimension=0, tiled=True
        ).astype(jnp.float32)

    sum_down = scattered(grad_down)
    sum_second = scattered(jnp.concatenate([grad_out, grad_gate_up], axis=1))
    small_sums = pack_small_sums(
        (
            grad_decay_up.reshape(rank, count, -1).transpose(1, 0, 2),
            grad_attn_gain,
            grad_mlp_gain,
            grad_decay_bias,
            grad_head_gain,
        ),
        count,
        rows,
    )
    sum_first = scattered(jnp.concatenate([grad_first, small_sums], axis=1))
    sum_query, sum_key, sum_value, sum_outgate, sum_decay_down = column_slices(
        sum_first, widths + (rank,)
    )
    sum_up, sum_attn, sum_mlp, sum_bias, sum_head = unpack_small(
        sum_first[:, wide + LANES :].reshape(-1), small_shapes
    )
    sum_out, sum_gate, sum_up_proj = column_slices(sum_second, (w_out.shape[1], hidden, hidden))
    return (
        block_output,
        input_grad,
        sum_attn,
        sum_query,
        sum_key,
        sum_value,
        sum_outgate,
        sum_decay_down,
        sum_up,
        sum_bias,
        sum_head,
        sum_out,
        sum_mlp,
        sum_gate,
        sum_up_proj,
        sum_down,
    )


def solution(mesh):
    return jax.shard_map(
        local,
        mesh=mesh,
        in_specs=(
            P("seq", None),
            P("seq", None),
            P("seq"),
            P("seq", None),
            P("seq", None),
            P("seq", None),
            P("seq", None),
            P("seq", None),
            P(None, "seq"),
            P("seq"),
            P("seq"),
            P("seq", None),
            P("seq"),
            P("seq", None),
            P("seq", None),
            P("seq", None),
        ),
        out_specs=(
            P("seq", None),
            P("seq", None),
            P("seq"),
            P("seq", None),
            P("seq", None),
            P("seq", None),
            P("seq", None),
            P("seq", None),
            P(None, "seq"),
            P("seq"),
            P("seq"),
            P("seq", None),
            P("seq"),
            P("seq", None),
            P("seq", None),
            P("seq", None),
        ),
        check_vma=False,
    )
```

```python
import jax
import jax.numpy as jnp
from jax import lax
from jax.experimental import pallas as pl
from jax.experimental.pallas import tpu as pltpu
from jax.sharding import PartitionSpec as P

H = 4
DK = 128
VALUE_WIDTH = 256
GROUP = 64


EPS = 1e-05
GATE_NORM = 16.0
TOP_PRECISION = lax.Precision.HIGHEST


LANES = 128


def pack_small(pieces, rows):
    flat = jnp.concatenate([piece.reshape(-1) for piece in pieces])
    return jnp.pad(flat, (0, rows * LANES - flat.shape[0])).reshape(rows, LANES)


def pack_small_sums(pieces, devices, rows):
    flat = jnp.concatenate([piece.reshape(devices, -1) for piece in pieces], axis=1)
    flat = jnp.pad(flat, ((0, 0), (0, rows * LANES - flat.shape[1])))
    return flat.reshape(devices * rows, LANES)


def unpack_small(flat, shapes):
    pieces, at = [], 0
    for shape in shapes:
        size = 1
        for extent in shape:
            size *= extent
        pieces.append(flat[..., at : at + size].reshape(flat.shape[:-1] + shape))
        at += size
    return pieces


def column_slices(array, widths):
    pieces, at = [], 0
    for width in widths:
        pieces.append(array[:, at : at + width])
        at += width
    return pieces


def three_pieces(value):
    high = value.astype(jnp.bfloat16)
    rest = value - high.astype(jnp.float32)
    middle = rest.astype(jnp.bfloat16)
    low = (rest - middle.astype(jnp.float32)).astype(jnp.bfloat16)
    return jnp.stack([high, middle, low])


def neighbour_ring(count):
    if count % 8:
        return tuple(range(count))
    levels, order = count // 8, []
    for column, chip in enumerate((0, 1, 3, 2)):
        climb = range(levels) if column % 2 == 0 else range(levels - 1, -1, -1)
        for level in climb:
            order += [8 * level + 2 * chip, 8 * level + 2 * chip + 1]
    return tuple(order)


def in_vmem():
    return pl.BlockSpec(memory_space=pltpu.VMEM)


def prefix_body(states, logs, out):
    count = states.shape[0]
    carried = jnp.zeros(states.shape[1:], jnp.float32)
    for device in range(count):
        out[device] = carried.astype(out.dtype)
        fading = jnp.exp(logs[device].astype(jnp.float32).sum(axis=-1, keepdims=True))
        carried = fading * carried + states[device].astype(jnp.float32)


def suffix_body(states, logs, out):
    count = states.shape[0]
    carried = jnp.zeros(states.shape[1:], jnp.float32)
    for device in range(count - 1, -1, -1):
        out[device] = carried.astype(out.dtype)
        fading = jnp.exp(logs[device].astype(jnp.float32).sum(axis=-1, keepdims=True))
        carried = fading * carried + states[device].astype(jnp.float32)


def scan_devices(body, states, logs):
    return pl.pallas_call(
        body,
        out_shape=jax.ShapeDtypeStruct(states.shape, jnp.bfloat16),
        in_specs=[in_vmem(), in_vmem()],
        out_specs=in_vmem(),
    )(states, logs)


def exchange(array):
    return lax.all_to_all(array, "seq", 0, 0)


def grad_body(left, right, *rest, order, rows, small):
    out = rest[-1]
    result = lax.dot_general(
        left[...], right[...], (((0,), (0,)), ((), ())), preferred_element_type=jnp.float32
    )
    for place, device in enumerate(order):
        out[place * rows : (place + 1) * rows, :] = result[
            device * rows : (device + 1) * rows, :
        ].astype(out.dtype)
    if small:
        sums = rest[0]

        @pl.when(pl.program_id(0) == pl.num_programs(0) - 1)
        def _():
            for place, device in enumerate(order):
                out[place * rows : (place + 1) * rows, out.shape[1] - LANES :] = sums[
                    device * rows : (device + 1) * rows, :
                ].astype(out.dtype)


def grad_into(left, right, order, buffer, total, start, block, sums=None):
    tokens, height = left.shape
    rows = height // len(order)
    first = start // block
    steps = pl.cdiv(right.shape[1], block)
    operands = [left, right]
    specs = [
        pl.BlockSpec((tokens, height), lambda j: (0, 0)),
        pl.BlockSpec((tokens, block), lambda j: (0, j)),
    ]
    if sums is not None:
        operands.append(sums)
        specs.append(pl.BlockSpec(sums.shape, lambda j: (0, 0)))
    aliases = {}
    if buffer is not None:
        aliases = {len(operands): 0}
        operands.append(buffer)
        specs.append(pl.BlockSpec(memory_space=pl.ANY))

    def body(*refs):
        grad_body(*refs, order=order, rows=rows, small=sums is not None)

    return pl.pallas_call(
        body,
        grid=(steps,),
        in_specs=specs,
        out_specs=pl.BlockSpec((height, block), lambda j: (0, j + first)),
        out_shape=jax.ShapeDtypeStruct((height, total), jnp.bfloat16),
        input_output_aliases=aliases,
    )(*operands)


def matmul(left_side, right_side):
    return jnp.dot(left_side, right_side, preferred_element_type=jnp.float32)


def times_back(left_side, right_side):
    return lax.dot_general(
        left_side, right_side, (((1,), (1,)), ((), ())), preferred_element_type=jnp.float32
    )


def outer_sum(left_side, right_side):
    return lax.dot_general(
        left_side, right_side, (((0,), (0,)), ((), ())), preferred_element_type=jnp.float32
    )


def rms_norm(matrix, gain):
    scaling = lax.rsqrt(jnp.mean(matrix * matrix, axis=-1, keepdims=True) + EPS)
    return matrix * scaling * gain


def swiglu(gate_pre, up_pre):
    return jax.nn.silu(gate_pre) * up_pre


def split_into_heads(matrix, columns):
    return matrix.reshape(matrix.shape[0] // GROUP, GROUP, H, columns).transpose(2, 0, 1, 3)


def from_heads(blocks):
    return blocks.transpose(1, 2, 0, 3).reshape(
        blocks.shape[1] * blocks.shape[2], blocks.shape[0] * blocks.shape[3]
    )


def to_front(tensor):
    return jnp.moveaxis(tensor, 1, 0)


def group_pass(query_blocks, key_blocks, value_blocks, decay_blocks, initial):
    inner = jnp.cumsum(decay_blocks, axis=2)
    ending = inner[:, :, -1:, :]
    query_in = query_blocks * jnp.exp(inner)
    key_in = key_blocks * jnp.exp(-inner)
    key_end = key_blocks * jnp.exp(ending - inner)
    length = query_blocks.shape[2]
    causal = jnp.tril(jnp.ones((length, length), jnp.float32))
    scores = jnp.einsum("hnck,hnsk->hncs", query_in, key_in, precision=TOP_PRECISION) * causal
    within = jnp.einsum("hncs,hnsv->hncv", scores, value_blocks, precision=TOP_PRECISION)

    def advance(carried_state, sequence_segments):
        query_segment, key_segment, value_segment, fading_factor = sequence_segments
        block_result = jnp.einsum(
            "waq,wqo->wao", query_segment, carried_state, precision=TOP_PRECISION
        )
        carried_state = fading_factor[:, 0, :, None] * carried_state + jnp.einsum(
            "fjb,fjq->fbq", key_segment, value_segment, precision=TOP_PRECISION
        )
        return (carried_state, block_result)

    final, across_pieces = lax.scan(
        advance,
        initial,
        (to_front(query_in), to_front(key_end), to_front(value_blocks), to_front(jnp.exp(ending))),
    )
    return (within + to_front(across_pieces), final)


def post_gate(mixer, outgate, head_gain):
    tokens_here = mixer.shape[0]
    per_head = mixer.reshape(tokens_here, H, VALUE_WIDTH)
    normed = rms_norm(per_head, head_gain).reshape(tokens_here, H * VALUE_WIDTH)
    return normed * outgate * jax.nn.sigmoid(outgate)


def local_pass(query, keys, values, decay_logit):
    log_decay = jax.nn.log_sigmoid(decay_logit) / GATE_NORM
    query_blocks = split_into_heads(query, DK)
    decay_blocks = split_into_heads(log_decay, DK)
    zero_state = jnp.zeros((H, DK, VALUE_WIDTH), jnp.float32)
    local_out, local_state = group_pass(
        query_blocks,
        split_into_heads(keys, DK),
        split_into_heads(values, VALUE_WIDTH),
        decay_blocks,
        zero_state,
    )
    layout = decay_blocks.shape
    cumulative = jnp.cumsum(
        decay_blocks.reshape(layout[0], layout[1] * layout[2], layout[3]), axis=1
    ).reshape(layout)
    log_fading = cumulative[:, -1, -1, :]
    query_fading = query_blocks * jnp.exp(cumulative)
    return (query_fading, log_fading, local_out, local_state)


def finish(sequence_segments, incoming_state):
    query_fading, log_fading, local_out, local_state = sequence_segments
    across_pieces = jnp.einsum(
        "qwxg,qgf->qwxf", query_fading, incoming_state, precision=TOP_PRECISION
    )
    return (
        from_heads(local_out + across_pieces),
        jnp.exp(log_fading)[:, :, None] * incoming_state + local_state,
    )


def local(
    block_input,
    cotangent,
    attn_gain,
    w_query,
    w_key,
    w_value,
    w_outgate,
    w_decay_down,
    w_decay_up,
    decay_bias,
    head_gain,
    w_out,
    mlp_gain,
    w_gate,
    w_up,
    w_down,
):
    count = lax.axis_size("seq")
    rows = w_query.shape[0]
    key_width, value_width, rank = (w_query.shape[1], w_value.shape[1], w_decay_down.shape[1])
    hidden = w_gate.shape[1]
    small_shapes = (w_decay_up.shape, attn_gain.shape, mlp_gain.shape, decay_bias.shape, head_gain.shape)
    first = jnp.concatenate(
        [
            w_query,
            w_key,
            w_value,
            w_outgate,
            jnp.pad(w_decay_down, ((0, 0), (0, LANES - rank))),
            pack_small((w_decay_up, attn_gain, mlp_gain, decay_bias, head_gain), rows),
        ],
        axis=1,
    )
    first = lax.all_gather(first, "seq", axis=0, tiled=True)
    second = jnp.concatenate([w_out, w_gate, w_up], axis=1)
    second = lax.all_gather(second, "seq", axis=0, tiled=True)
    down_full = lax.all_gather(w_down, "seq", axis=0, tiled=True)
    widths = (key_width, key_width, value_width, value_width)
    wide = 2 * key_width + 2 * value_width
    projection = first[:, : wide + LANES]
    small = first[:, wide + LANES :].reshape(count, rows * LANES)
    up_pieces, attn_full, mlp_full_gain, bias_full, head_full = unpack_small(small, small_shapes)
    decay_up_full = up_pieces.transpose(1, 0, 2).reshape(rank, key_width)
    attn_full, mlp_full_gain, bias_full, head_full = (
        piece.reshape(-1).astype(jnp.float32) for piece in (attn_full, mlp_full_gain, bias_full, head_full)
    )
    out_full = second[:, : w_out.shape[1]]
    gate_up = second[:, w_out.shape[1] :]
    scaling = DK ** (-0.5)
    normed, norm_back = jax.vjp(rms_norm, block_input, attn_full)
    normed_in = normed.astype(jnp.bfloat16)
    query, keys, values, outgate, low_rank = column_slices(
        matmul(normed_in, projection), widths + (rank,)
    )
    query = query * scaling
    low_rank = low_rank.astype(jnp.bfloat16)
    decay_logit = matmul(low_rank, decay_up_full) + bias_full
    sequence_segments, local_back = jax.vjp(local_pass, query, keys, values, decay_logit)
    chunk = key_width // count
    state = sequence_segments[3].reshape(key_width, VALUE_WIDTH).astype(jnp.bfloat16)
    log_pieces = three_pieces(sequence_segments[1].reshape(-1)).T
    log_pieces = jnp.pad(log_pieces, ((0, 0), (0, LANES - 3)))
    arrived = exchange(
        jnp.concatenate([state, log_pieces], axis=1).reshape(count, chunk, VALUE_WIDTH + LANES)
    )
    logs = arrived[:, :, VALUE_WIDTH:]
    before = exchange(scan_devices(prefix_body, arrived[:, :, :VALUE_WIDTH], logs))
    incoming_state = before.reshape(H, DK, VALUE_WIDTH).astype(jnp.float32)
    mixer, state_after = finish(sequence_segments, incoming_state)
    gated_full, post_back = jax.vjp(post_gate, mixer, outgate, head_full)
    gated = gated_full.astype(jnp.bfloat16)
    hidden_state = block_input + matmul(gated, out_full)
    mlp_full, mlp_back = jax.vjp(rms_norm, hidden_state, mlp_full_gain)
    mlp_normed = mlp_full.astype(jnp.bfloat16)
    gate_pre, up_pre = column_slices(matmul(mlp_normed, gate_up), (hidden, hidden))
    activ_full, activ_back = jax.vjp(swiglu, gate_pre, up_pre)
    activ = activ_full.astype(jnp.bfloat16)
    block_output = hidden_state + matmul(activ, down_full)
    cot_in = cotangent.astype(jnp.bfloat16)
    d_activ = times_back(cot_in, down_full)
    d_gate_full, d_up_full = activ_back(d_activ)
    d_gate = d_gate_full.astype(jnp.bfloat16)
    d_up = d_up_full.astype(jnp.bfloat16)
    d_gate_up = jnp.concatenate([d_gate, d_up], axis=1)
    d_mlp_normed = times_back(d_gate_up, gate_up)
    d_hidden_norm, grad_mlp_gain = mlp_back(d_mlp_normed)
    d_hidden = cotangent + d_hidden_norm
    d_hidden_in = d_hidden.astype(jnp.bfloat16)
    d_gated = times_back(d_hidden_in, out_full)
    mixer_gradient, d_outgate, grad_head_gain = post_back(d_gated)
    state_gradient = jnp.einsum(
        "ryfm,ryfj->rmj",
        sequence_segments[0],
        split_into_heads(mixer_gradient, VALUE_WIDTH),
        precision=TOP_PRECISION,
    )
    arrived_back = exchange(
        state_gradient.reshape(count, chunk, VALUE_WIDTH).astype(jnp.bfloat16)
    )
    after = exchange(scan_devices(suffix_body, arrived_back, logs))
    after = after.reshape(H, DK, VALUE_WIDTH).astype(jnp.float32)
    finish_value, finish_back = jax.vjp(finish, sequence_segments, incoming_state)
    d_pieces, d_incoming = finish_back((mixer_gradient, after))
    d_query, d_keys, d_values, d_logit = local_back(d_pieces)
    grad_decay_bias = jnp.sum(d_logit, axis=0)
    d_logit_in = d_logit.astype(jnp.bfloat16)
    grad_decay_up = outer_sum(low_rank, d_logit_in)
    d_low = times_back(d_logit_in, decay_up_full).astype(jnp.bfloat16)
    d_first = jnp.concatenate(
        [
            (d_query * scaling).astype(jnp.bfloat16),
            d_keys.astype(jnp.bfloat16),
            d_values.astype(jnp.bfloat16),
            d_outgate.astype(jnp.bfloat16),
            jnp.pad(d_low, ((0, 0), (0, 2 * LANES - rank))),
        ],
        axis=1,
    )
    d_normed = times_back(d_first, first)
    d_input_norm, grad_attn_gain = norm_back(d_normed)
    input_grad = d_hidden + d_input_norm

    small_sums = pack_small_sums(
        (
            grad_decay_up.reshape(rank, count, -1).transpose(1, 0, 2),
            grad_attn_gain,
            grad_mlp_gain,
            grad_decay_bias,
            grad_head_gain,
        ),
        count,
        rows,
    )
    order = neighbour_ring(count)
    down_rows = w_down.shape[0]
    down_order = order if down_rows % 8 == 0 else tuple(range(count))

    def scattered(partial, devices):
        return lax.psum_scatter(
            partial,
            "seq",
            scatter_dimension=0,
            tiled=True,
            axis_index_groups=None if devices == tuple(range(count)) else [list(devices)],
        ).astype(jnp.float32)

    if down_rows % 8 == 0:
        grad_down = grad_into(activ, cot_in, down_order, None, w_down.shape[1], 0, 256)
    else:
        grad_down = outer_sum(activ, cot_in).astype(jnp.bfloat16)
    sum_down = scattered(grad_down, down_order)
    width = wide + 2 * LANES + w_out.shape[1] + 2 * hidden
    sums = grad_into(mlp_normed, d_gate_up, order, None, width, 0, 512)
    sums = grad_into(gated, d_hidden_in, order, sums, width, 2 * hidden, 512)
    sums = grad_into(
        normed_in, d_first, order, sums, width, 2 * hidden + w_out.shape[1], 256, small_sums
    )
    sums = scattered(sums, order)
    sum_gate, sum_up_proj, sum_out, sum_first = column_slices(
        sums, (hidden, hidden, w_out.shape[1], wide + 2 * LANES)
    )
    sum_query, sum_key, sum_value, sum_outgate, sum_decay_down = column_slices(
        sum_first, widths + (rank,)
    )
    sum_up, sum_attn, sum_mlp, sum_bias, sum_head = unpack_small(
        sum_first[:, wide + LANES :].reshape(-1), small_shapes
    )
    return (
        block_output,
        input_grad,
        sum_attn,
        sum_query,
        sum_key,
        sum_value,
        sum_outgate,
        sum_decay_down,
        sum_up,
        sum_bias,
        sum_head,
        sum_out,
        sum_mlp,
        sum_gate,
        sum_up_proj,
        sum_down,
    )


def solution(mesh):
    return jax.shard_map(
        local,
        mesh=mesh,
        in_specs=(
            P("seq", None),
            P("seq", None),
            P("seq"),
            P("seq", None),
            P("seq", None),
            P("seq", None),
            P("seq", None),
            P("seq", None),
            P(None, "seq"),
            P("seq"),
            P("seq"),
            P("seq", None),
            P("seq"),
            P("seq", None),
            P("seq", None),
            P("seq", None),
        ),
        out_specs=(
            P("seq", None),
            P("seq", None),
            P("seq"),
            P("seq", None),
            P("seq", None),
            P("seq", None),
            P("seq", None),
            P("seq", None),
            P(None, "seq"),
            P("seq"),
            P("seq"),
            P("seq", None),
            P("seq"),
            P("seq", None),
            P("seq", None),
            P("seq", None),
        ),
        check_vma=False,
    )
```

```python
import jax
import jax.numpy as jnp
from jax import lax
from jax.experimental import pallas as pl
from jax.experimental.pallas import tpu as pltpu
from jax.sharding import PartitionSpec as P

H = 4
DK = 128
VALUE_WIDTH = 256
GROUP = 64


EPS = 1e-05
GATE_NORM = 16.0
TOP_PRECISION = lax.Precision.HIGHEST


LANES = 128


def pack_small(pieces, rows):
    flat = jnp.concatenate([piece.reshape(-1) for piece in pieces])
    return jnp.pad(flat, (0, rows * LANES - flat.shape[0])).reshape(rows, LANES)


def pack_small_sums(pieces, devices, rows):
    flat = jnp.concatenate([piece.reshape(devices, -1) for piece in pieces], axis=1)
    flat = jnp.pad(flat, ((0, 0), (0, rows * LANES - flat.shape[1])))
    return flat.reshape(devices * rows, LANES)


def unpack_small(flat, shapes):
    pieces, at = [], 0
    for shape in shapes:
        size = 1
        for extent in shape:
            size *= extent
        pieces.append(flat[..., at : at + size].reshape(flat.shape[:-1] + shape))
        at += size
    return pieces


def column_slices(array, widths):
    pieces, at = [], 0
    for width in widths:
        pieces.append(array[:, at : at + width])
        at += width
    return pieces


def three_pieces(value):
    high = value.astype(jnp.bfloat16)
    rest = value - high.astype(jnp.float32)
    middle = rest.astype(jnp.bfloat16)
    low = (rest - middle.astype(jnp.float32)).astype(jnp.bfloat16)
    return jnp.stack([high, middle, low])


def neighbour_ring(count):
    if count % 8:
        return tuple(range(count))
    levels, order = count // 8, []
    for column, chip in enumerate((0, 1, 3, 2)):
        climb = range(levels) if column % 2 == 0 else range(levels - 1, -1, -1)
        for level in climb:
            order += [8 * level + 2 * chip, 8 * level + 2 * chip + 1]
    return tuple(order)


def in_vmem():
    return pl.BlockSpec(memory_space=pltpu.VMEM)


def prefix_body(states, logs, out):
    count = states.shape[0]
    carried = jnp.zeros(states.shape[1:], jnp.float32)
    for device in range(count):
        out[device] = carried.astype(out.dtype)
        fading = jnp.exp(logs[device].astype(jnp.float32).sum(axis=-1, keepdims=True))
        carried = fading * carried + states[device].astype(jnp.float32)


def suffix_body(states, logs, out):
    count = states.shape[0]
    carried = jnp.zeros(states.shape[1:], jnp.float32)
    for device in range(count - 1, -1, -1):
        out[device] = carried.astype(out.dtype)
        fading = jnp.exp(logs[device].astype(jnp.float32).sum(axis=-1, keepdims=True))
        carried = fading * carried + states[device].astype(jnp.float32)


def scan_devices(body, states, logs):
    return pl.pallas_call(
        body,
        out_shape=jax.ShapeDtypeStruct(states.shape, jnp.bfloat16),
        in_specs=[in_vmem(), in_vmem()],
        out_specs=in_vmem(),
    )(states, logs)


def exchange(array):
    return lax.all_to_all(array, "seq", 0, 0)


PLANE = 8
OFFSETS = (0, 2, 4, 6)


def plane_groups(count):
    return [list(range(start, start + PLANE)) for start in range(0, count, PLANE)]


def level_groups(count):
    return [list(range(place, count, PLANE)) for place in range(PLANE)]


def swapped(array, offset):
    count = lax.axis_size("seq")
    return lax.ppermute(array, "seq", [(device, device ^ offset) for device in range(count)])


def plane_gather(array):
    same = [array] + [swapped(array, offset) for offset in OFFSETS[1:]]
    return jnp.concatenate(same + [swapped(part, 1) for part in same], axis=0)


def plane_scatter(partial):
    half = partial.shape[0] // 2
    rows = half // len(OFFSETS)
    joined = partial[:half] + swapped(partial[half:].astype(jnp.bfloat16), 1).astype(jnp.float32)
    total = joined[:rows]
    for place, offset in enumerate(OFFSETS[1:], 1):
        piece = joined[place * rows : (place + 1) * rows].astype(jnp.bfloat16)
        total = total + swapped(piece, offset).astype(jnp.float32)
    return total


def to_units(weight, levels, padded):
    rows, hidden = weight.shape
    width = hidden // (levels * PLANE)
    parts = weight.reshape(rows, levels, PLANE, width).transpose(2, 0, 1, 3)
    parts = parts.reshape(PLANE, rows, levels * width)
    return jnp.pad(parts, ((0, 0), (0, 0), (0, padded - levels * width)))


def from_units(parts, levels, hidden):
    rows = parts.shape[1]
    width = hidden // (levels * PLANE)
    parts = parts[:, :, : levels * width].reshape(PLANE, rows, levels, width)
    return parts.transpose(1, 2, 0, 3).reshape(rows, hidden)


def grad_body(left, right, *rest, order, rows, small):
    out = rest[-1]
    result = lax.dot_general(
        left[...], right[...], (((0,), (0,)), ((), ())), preferred_element_type=jnp.float32
    )
    for place, device in enumerate(order):
        out[place * rows : (place + 1) * rows, :] = result[
            device * rows : (device + 1) * rows, :
        ].astype(out.dtype)
    if small:
        sums = rest[0]

        @pl.when(pl.program_id(0) == pl.num_programs(0) - 1)
        def _():
            for place, device in enumerate(order):
                out[place * rows : (place + 1) * rows, out.shape[1] - LANES :] = sums[
                    device * rows : (device + 1) * rows, :
                ].astype(out.dtype)


def grad_into(left, right, order, buffer, total, start, block, sums=None):
    tokens, height = left.shape
    rows = height // len(order)
    first = start // block
    steps = pl.cdiv(right.shape[1], block)
    operands = [left, right]
    specs = [
        pl.BlockSpec((tokens, height), lambda j: (0, 0)),
        pl.BlockSpec((tokens, block), lambda j: (0, j)),
    ]
    if sums is not None:
        operands.append(sums)
        specs.append(pl.BlockSpec(sums.shape, lambda j: (0, 0)))
    aliases = {}
    if buffer is not None:
        aliases = {len(operands): 0}
        operands.append(buffer)
        specs.append(pl.BlockSpec(memory_space=pl.ANY))

    def body(*refs):
        grad_body(*refs, order=order, rows=rows, small=sums is not None)

    return pl.pallas_call(
        body,
        grid=(steps,),
        in_specs=specs,
        out_specs=pl.BlockSpec((height, block), lambda j: (0, j + first)),
        out_shape=jax.ShapeDtypeStruct((height, total), jnp.bfloat16),
        input_output_aliases=aliases,
    )(*operands)


def matmul(left_side, right_side):
    return jnp.dot(left_side, right_side, preferred_element_type=jnp.float32)


def times_back(left_side, right_side):
    return lax.dot_general(
        left_side, right_side, (((1,), (1,)), ((), ())), preferred_element_type=jnp.float32
    )


def outer_sum(left_side, right_side):
    return lax.dot_general(
        left_side, right_side, (((0,), (0,)), ((), ())), preferred_element_type=jnp.float32
    )


def rms_norm(matrix, gain):
    scaling = lax.rsqrt(jnp.mean(matrix * matrix, axis=-1, keepdims=True) + EPS)
    return matrix * scaling * gain


def swiglu(gate_pre, up_pre):
    return jax.nn.silu(gate_pre) * up_pre


def split_into_heads(matrix, columns):
    return matrix.reshape(matrix.shape[0] // GROUP, GROUP, H, columns).transpose(2, 0, 1, 3)


def from_heads(blocks):
    return blocks.transpose(1, 2, 0, 3).reshape(
        blocks.shape[1] * blocks.shape[2], blocks.shape[0] * blocks.shape[3]
    )


def to_front(tensor):
    return jnp.moveaxis(tensor, 1, 0)


def group_pass(query_blocks, key_blocks, value_blocks, decay_blocks, initial):
    inner = jnp.cumsum(decay_blocks, axis=2)
    ending = inner[:, :, -1:, :]
    query_in = query_blocks * jnp.exp(inner)
    key_in = key_blocks * jnp.exp(-inner)
    key_end = key_blocks * jnp.exp(ending - inner)
    length = query_blocks.shape[2]
    causal = jnp.tril(jnp.ones((length, length), jnp.float32))
    scores = jnp.einsum("hnck,hnsk->hncs", query_in, key_in, precision=TOP_PRECISION) * causal
    within = jnp.einsum("hncs,hnsv->hncv", scores, value_blocks, precision=TOP_PRECISION)

    def advance(carried_state, sequence_segments):
        query_segment, key_segment, value_segment, fading_factor = sequence_segments
        block_result = jnp.einsum(
            "waq,wqo->wao", query_segment, carried_state, precision=TOP_PRECISION
        )
        carried_state = fading_factor[:, 0, :, None] * carried_state + jnp.einsum(
            "fjb,fjq->fbq", key_segment, value_segment, precision=TOP_PRECISION
        )
        return (carried_state, block_result)

    final, across_pieces = lax.scan(
        advance,
        initial,
        (to_front(query_in), to_front(key_end), to_front(value_blocks), to_front(jnp.exp(ending))),
    )
    return (within + to_front(across_pieces), final)


def post_gate(mixer, outgate, head_gain):
    tokens_here = mixer.shape[0]
    per_head = mixer.reshape(tokens_here, H, VALUE_WIDTH)
    normed = rms_norm(per_head, head_gain).reshape(tokens_here, H * VALUE_WIDTH)
    return normed * outgate * jax.nn.sigmoid(outgate)


def local_pass(query, keys, values, decay_logit):
    log_decay = jax.nn.log_sigmoid(decay_logit) / GATE_NORM
    query_blocks = split_into_heads(query, DK)
    decay_blocks = split_into_heads(log_decay, DK)
    zero_state = jnp.zeros((H, DK, VALUE_WIDTH), jnp.float32)
    local_out, local_state = group_pass(
        query_blocks,
        split_into_heads(keys, DK),
        split_into_heads(values, VALUE_WIDTH),
        decay_blocks,
        zero_state,
    )
    layout = decay_blocks.shape
    cumulative = jnp.cumsum(
        decay_blocks.reshape(layout[0], layout[1] * layout[2], layout[3]), axis=1
    ).reshape(layout)
    log_fading = cumulative[:, -1, -1, :]
    query_fading = query_blocks * jnp.exp(cumulative)
    return (query_fading, log_fading, local_out, local_state)


def finish(sequence_segments, incoming_state):
    query_fading, log_fading, local_out, local_state = sequence_segments
    across_pieces = jnp.einsum(
        "qwxg,qgf->qwxf", query_fading, incoming_state, precision=TOP_PRECISION
    )
    return (
        from_heads(local_out + across_pieces),
        jnp.exp(log_fading)[:, :, None] * incoming_state + local_state,
    )


def local(
    block_input,
    cotangent,
    attn_gain,
    w_query,
    w_key,
    w_value,
    w_outgate,
    w_decay_down,
    w_decay_up,
    decay_bias,
    head_gain,
    w_out,
    mlp_gain,
    w_gate,
    w_up,
    w_down,
):
    count = lax.axis_size("seq")
    rows = w_query.shape[0]
    key_width, value_width, rank = (w_query.shape[1], w_value.shape[1], w_decay_down.shape[1])
    hidden = w_gate.shape[1]
    small_shapes = (w_decay_up.shape, attn_gain.shape, mlp_gain.shape, decay_bias.shape, head_gain.shape)
    first = jnp.concatenate(
        [
            w_query,
            w_key,
            w_value,
            w_outgate,
            jnp.pad(w_decay_down, ((0, 0), (0, LANES - rank))),
            pack_small((w_decay_up, attn_gain, mlp_gain, decay_bias, head_gain), rows),
            w_out,
        ],
        axis=1,
    )
    first = lax.all_gather(first, "seq", axis=0, tiled=True)
    levels = count // PLANE
    planes, columns = (plane_groups(count), level_groups(count))
    units = levels * w_down.shape[0]
    padded = -(-units // LANES) * LANES
    gate_up = jnp.concatenate([to_units(w_gate, levels, padded), to_units(w_up, levels, padded)], axis=2)
    gate_up = lax.all_to_all(gate_up, "seq", 0, 0, axis_index_groups=planes)
    gate_up = gate_up.reshape(PLANE * rows, 2 * padded)
    gate_up = lax.all_gather(gate_up, "seq", axis=0, tiled=True, axis_index_groups=columns)
    down = lax.all_gather(w_down, "seq", axis=0, tiled=True, axis_index_groups=columns)
    down = jnp.pad(down, ((0, padded - units), (0, 0)))
    cot_in, first = lax.optimization_barrier((cotangent.astype(jnp.bfloat16), first))
    cot_plane = plane_gather(cot_in)
    widths = (key_width, key_width, value_width, value_width)
    wide = 2 * key_width + 2 * value_width
    projection = first[:, : wide + LANES]
    small = first[:, wide + LANES : wide + 2 * LANES].reshape(count, rows * LANES)
    up_pieces, attn_full, mlp_full_gain, bias_full, head_full = unpack_small(small, small_shapes)
    decay_up_full = up_pieces.transpose(1, 0, 2).reshape(rank, key_width)
    attn_full, mlp_full_gain, bias_full, head_full = (
        piece.reshape(-1).astype(jnp.float32) for piece in (attn_full, mlp_full_gain, bias_full, head_full)
    )
    out_full = first[:, wide + 2 * LANES :]
    scaling = DK ** (-0.5)
    normed, norm_back = jax.vjp(rms_norm, block_input, attn_full)
    normed_in = normed.astype(jnp.bfloat16)
    query, keys, values, outgate, low_rank = column_slices(
        matmul(normed_in, projection), widths + (rank,)
    )
    query = query * scaling
    low_rank = low_rank.astype(jnp.bfloat16)
    decay_logit = matmul(low_rank, decay_up_full) + bias_full
    sequence_segments, local_back = jax.vjp(local_pass, query, keys, values, decay_logit)
    chunk = key_width // count
    state = sequence_segments[3].reshape(key_width, VALUE_WIDTH).astype(jnp.bfloat16)
    log_pieces = three_pieces(sequence_segments[1].reshape(-1)).T
    log_pieces = jnp.pad(log_pieces, ((0, 0), (0, LANES - 3)))
    arrived = exchange(
        jnp.concatenate([state, log_pieces], axis=1).reshape(count, chunk, VALUE_WIDTH + LANES)
    )
    logs = arrived[:, :, VALUE_WIDTH:]
    before = exchange(scan_devices(prefix_body, arrived[:, :, :VALUE_WIDTH], logs))
    incoming_state = before.reshape(H, DK, VALUE_WIDTH).astype(jnp.float32)
    mixer, state_after = finish(sequence_segments, incoming_state)
    gated_full, post_back = jax.vjp(post_gate, mixer, outgate, head_full)
    gated = gated_full.astype(jnp.bfloat16)
    hidden_state = block_input + matmul(gated, out_full)
    mlp_full, mlp_back = jax.vjp(rms_norm, hidden_state, mlp_full_gain)
    mlp_normed = mlp_full.astype(jnp.bfloat16)
    mlp_plane = plane_gather(mlp_normed)
    gate_pre, up_pre = column_slices(matmul(mlp_plane, gate_up), (padded, padded))
    activ_full, activ_back = jax.vjp(swiglu, gate_pre, up_pre)
    activ = activ_full.astype(jnp.bfloat16)
    d_activ = times_back(cot_plane, down)
    d_gate_full, d_up_full = activ_back(d_activ)
    d_gate_up = jnp.concatenate(
        [d_gate_full.astype(jnp.bfloat16), d_up_full.astype(jnp.bfloat16)], axis=1
    )
    d_mlp_normed = plane_scatter(times_back(d_gate_up, gate_up))
    block_output = hidden_state + plane_scatter(matmul(activ, down))

    def level_sum(partial):
        return lax.psum_scatter(
            partial.astype(jnp.bfloat16),
            "seq",
            scatter_dimension=0,
            tiled=True,
            axis_index_groups=columns,
        )

    sum_down = level_sum(outer_sum(activ, cot_plane)[:units]).astype(jnp.float32)
    sum_gate_up = level_sum(outer_sum(mlp_plane, d_gate_up)).reshape(PLANE, rows, 2 * padded)
    sum_gate_up = lax.all_to_all(sum_gate_up, "seq", 0, 0, axis_index_groups=planes)
    sum_gate_up = sum_gate_up.astype(jnp.float32)
    sum_gate = from_units(sum_gate_up[:, :, :padded], levels, hidden)
    sum_up_proj = from_units(sum_gate_up[:, :, padded:], levels, hidden)
    d_hidden_norm, grad_mlp_gain = mlp_back(d_mlp_normed)
    d_hidden = cotangent + d_hidden_norm
    d_hidden_in = d_hidden.astype(jnp.bfloat16)
    d_gated = times_back(d_hidden_in, out_full)
    mixer_gradient, d_outgate, grad_head_gain = post_back(d_gated)
    state_gradient = jnp.einsum(
        "ryfm,ryfj->rmj",
        sequence_segments[0],
        split_into_heads(mixer_gradient, VALUE_WIDTH),
        precision=TOP_PRECISION,
    )
    arrived_back = exchange(
        state_gradient.reshape(count, chunk, VALUE_WIDTH).astype(jnp.bfloat16)
    )
    after = exchange(scan_devices(suffix_body, arrived_back, logs))
    after = after.reshape(H, DK, VALUE_WIDTH).astype(jnp.float32)
    finish_value, finish_back = jax.vjp(finish, sequence_segments, incoming_state)
    d_pieces, d_incoming = finish_back((mixer_gradient, after))
    d_query, d_keys, d_values, d_logit = local_back(d_pieces)
    grad_decay_bias = jnp.sum(d_logit, axis=0)
    d_logit_in = d_logit.astype(jnp.bfloat16)
    grad_decay_up = outer_sum(low_rank, d_logit_in)
    d_low = times_back(d_logit_in, decay_up_full).astype(jnp.bfloat16)
    d_first = jnp.concatenate(
        [
            (d_query * scaling).astype(jnp.bfloat16),
            d_keys.astype(jnp.bfloat16),
            d_values.astype(jnp.bfloat16),
            d_outgate.astype(jnp.bfloat16),
            jnp.pad(d_low, ((0, 0), (0, 2 * LANES - rank))),
        ],
        axis=1,
    )
    d_normed = times_back(d_first, first[:, : wide + 2 * LANES])
    d_input_norm, grad_attn_gain = norm_back(d_normed)
    input_grad = d_hidden + d_input_norm

    small_sums = pack_small_sums(
        (
            grad_decay_up.reshape(rank, count, -1).transpose(1, 0, 2),
            grad_attn_gain,
            grad_mlp_gain,
            grad_decay_bias,
            grad_head_gain,
        ),
        count,
        rows,
    )
    order = neighbour_ring(count)
    def scattered(partial, devices):
        return lax.psum_scatter(
            partial,
            "seq",
            scatter_dimension=0,
            tiled=True,
            axis_index_groups=None if devices == tuple(range(count)) else [list(devices)],
        ).astype(jnp.float32)

    width = wide + 2 * LANES + w_out.shape[1]
    sums = grad_into(gated, d_hidden_in, order, None, width, 0, 512)
    sums = grad_into(normed_in, d_first, order, sums, width, w_out.shape[1], 256, small_sums)
    sums = scattered(sums, order)
    sum_out, sum_first = column_slices(sums, (w_out.shape[1], wide + 2 * LANES))
    sum_query, sum_key, sum_value, sum_outgate, sum_decay_down = column_slices(
        sum_first, widths + (rank,)
    )
    sum_up, sum_attn, sum_mlp, sum_bias, sum_head = unpack_small(
        sum_first[:, wide + LANES :].reshape(-1), small_shapes
    )
    return (
        block_output,
        input_grad,
        sum_attn,
        sum_query,
        sum_key,
        sum_value,
        sum_outgate,
        sum_decay_down,
        sum_up,
        sum_bias,
        sum_head,
        sum_out,
        sum_mlp,
        sum_gate,
        sum_up_proj,
        sum_down,
    )


def solution(mesh):
    return jax.shard_map(
        local,
        mesh=mesh,
        in_specs=(
            P("seq", None),
            P("seq", None),
            P("seq"),
            P("seq", None),
            P("seq", None),
            P("seq", None),
            P("seq", None),
            P("seq", None),
            P(None, "seq"),
            P("seq"),
            P("seq"),
            P("seq", None),
            P("seq"),
            P("seq", None),
            P("seq", None),
            P("seq", None),
        ),
        out_specs=(
            P("seq", None),
            P("seq", None),
            P("seq"),
            P("seq", None),
            P("seq", None),
            P("seq", None),
            P("seq", None),
            P("seq", None),
            P(None, "seq"),
            P("seq"),
            P("seq"),
            P("seq", None),
            P("seq"),
            P("seq", None),
            P("seq", None),
            P("seq", None),
        ),
        check_vma=False,
    )
```

```python
import jax
import jax.numpy as jnp
from jax import lax
from jax.experimental import pallas as pl
from jax.experimental.pallas import tpu as pltpu
from jax.sharding import PartitionSpec as P

H = 4
DK = 128
VALUE_WIDTH = 256
GROUP = 64


EPS = 1e-05
GATE_NORM = 16.0
TOP_PRECISION = lax.Precision.HIGHEST


LANES = 128


def pack_small(pieces, rows):
    flat = jnp.concatenate([piece.reshape(-1) for piece in pieces])
    return jnp.pad(flat, (0, rows * LANES - flat.shape[0])).reshape(rows, LANES)


def pack_small_sums(pieces, devices):
    flat = jnp.concatenate([piece.reshape(devices, -1) for piece in pieces], axis=1)
    return jnp.pad(flat, ((0, 0), (0, -flat.shape[1] % LANES)))


def unpack_small(flat, shapes):
    pieces, at = [], 0
    for shape in shapes:
        size = 1
        for extent in shape:
            size *= extent
        pieces.append(flat[..., at : at + size].reshape(flat.shape[:-1] + shape))
        at += size
    return pieces


def column_slices(array, widths):
    pieces, at = [], 0
    for width in widths:
        pieces.append(array[:, at : at + width])
        at += width
    return pieces


def three_pieces(value):
    high = value.astype(jnp.bfloat16)
    rest = value - high.astype(jnp.float32)
    middle = rest.astype(jnp.bfloat16)
    low = (rest - middle.astype(jnp.float32)).astype(jnp.bfloat16)
    return jnp.stack([high, middle, low])


def neighbour_ring(count):
    if count % 8:
        return tuple(range(count))
    levels, order = count // 8, []
    for column, chip in enumerate((0, 1, 3, 2)):
        climb = range(levels) if column % 2 == 0 else range(levels - 1, -1, -1)
        for level in climb:
            order += [8 * level + 2 * chip, 8 * level + 2 * chip + 1]
    return tuple(order)


def in_vmem():
    return pl.BlockSpec(memory_space=pltpu.VMEM)


def prefix_body(states, logs, out):
    count = states.shape[0]
    carried = jnp.zeros(states.shape[1:], jnp.float32)
    for device in range(count):
        out[device] = carried.astype(out.dtype)
        fading = jnp.exp(logs[device].astype(jnp.float32).sum(axis=-1, keepdims=True))
        carried = fading * carried + states[device].astype(jnp.float32)


def suffix_body(states, logs, out):
    count = states.shape[0]
    carried = jnp.zeros(states.shape[1:], jnp.float32)
    for device in range(count - 1, -1, -1):
        out[device] = carried.astype(out.dtype)
        fading = jnp.exp(logs[device].astype(jnp.float32).sum(axis=-1, keepdims=True))
        carried = fading * carried + states[device].astype(jnp.float32)


def scan_devices(body, states, logs):
    return pl.pallas_call(
        body,
        out_shape=jax.ShapeDtypeStruct(states.shape, jnp.bfloat16),
        in_specs=[in_vmem(), in_vmem()],
        out_specs=in_vmem(),
    )(states, logs)


def exchange(array):
    return lax.all_to_all(array, "seq", 0, 0)


PLANE = 8
OFFSETS = (0, 2, 4, 6)


def plane_groups(count):
    return [list(range(start, start + PLANE)) for start in range(0, count, PLANE)]


def level_groups(count):
    return [list(range(place, count, PLANE)) for place in range(PLANE)]


def swapped(array, offset):
    count = lax.axis_size("seq")
    return lax.ppermute(array, "seq", [(device, device ^ offset) for device in range(count)])


def plane_gather(array):
    same = [array] + [swapped(array, offset) for offset in OFFSETS[1:]]
    return jnp.concatenate(same + [swapped(part, 1) for part in same], axis=0)


def plane_scatter(partial):
    half = partial.shape[0] // 2
    rows = half // len(OFFSETS)
    joined = partial[:half] + swapped(partial[half:].astype(jnp.bfloat16), 1).astype(jnp.float32)
    total = joined[:rows]
    for place, offset in enumerate(OFFSETS[1:], 1):
        piece = joined[place * rows : (place + 1) * rows].astype(jnp.bfloat16)
        total = total + swapped(piece, offset).astype(jnp.float32)
    return total


def to_units(weight, levels, padded):
    rows, hidden = weight.shape
    width = hidden // (levels * PLANE)
    parts = weight.reshape(rows, levels, PLANE, width).transpose(2, 0, 1, 3)
    parts = parts.reshape(PLANE, rows, levels * width)
    return jnp.pad(parts, ((0, 0), (0, 0), (0, padded - levels * width)))


def from_units(parts, levels, hidden):
    rows = parts.shape[1]
    width = hidden // (levels * PLANE)
    parts = parts[:, :, : levels * width].reshape(PLANE, rows, levels, width)
    return parts.transpose(1, 2, 0, 3).reshape(rows, hidden)


def grad_body(left, right, *rest):
    out = rest[-1]
    out[...] = lax.dot_general(
        left[...], right[...], (((0,), (0,)), ((), ())), preferred_element_type=jnp.float32
    ).astype(out.dtype)


def grad_into(left, right, buffer, total, start, block):
    tokens, height = left.shape
    first = start // block
    operands = [left, right]
    specs = [
        pl.BlockSpec((tokens, height), lambda j: (0, 0)),
        pl.BlockSpec((tokens, block), lambda j: (0, j)),
    ]
    aliases = {}
    if buffer is not None:
        aliases = {len(operands): 0}
        operands.append(buffer)
        specs.append(pl.BlockSpec(memory_space=pl.ANY))
    return pl.pallas_call(
        grad_body,
        grid=(pl.cdiv(right.shape[1], block),),
        in_specs=specs,
        out_specs=pl.BlockSpec((height, block), lambda j: (0, j + first)),
        out_shape=jax.ShapeDtypeStruct((height, total), jnp.bfloat16),
        input_output_aliases=aliases,
    )(*operands)


def with_partner(array):
    return jnp.concatenate([array, swapped(array, 1)], axis=0)


def own_columns(array, chips, parity, rows):
    width = array.shape[1]
    column = jnp.arange(width // 2)
    place = jnp.asarray(chips, jnp.int32)[column // rows]
    source = (2 * place + parity) * rows + column % rows
    pick = jnp.arange(width)[:, None] == source[None, :]
    return jnp.dot(array, pick.astype(array.dtype), preferred_element_type=array.dtype)


def matmul(left_side, right_side):
    return jnp.dot(left_side, right_side, preferred_element_type=jnp.float32)


def times_back(left_side, right_side):
    return lax.dot_general(
        left_side, right_side, (((1,), (1,)), ((), ())), preferred_element_type=jnp.float32
    )


def outer_sum(left_side, right_side):
    return lax.dot_general(
        left_side, right_side, (((0,), (0,)), ((), ())), preferred_element_type=jnp.float32
    )


def rms_norm(matrix, gain):
    scaling = lax.rsqrt(jnp.mean(matrix * matrix, axis=-1, keepdims=True) + EPS)
    return matrix * scaling * gain


def swiglu(gate_pre, up_pre):
    return jax.nn.silu(gate_pre) * up_pre


def split_into_heads(matrix, columns):
    return matrix.reshape(matrix.shape[0] // GROUP, GROUP, H, columns).transpose(2, 0, 1, 3)


def from_heads(blocks):
    return blocks.transpose(1, 2, 0, 3).reshape(
        blocks.shape[1] * blocks.shape[2], blocks.shape[0] * blocks.shape[3]
    )


def to_front(tensor):
    return jnp.moveaxis(tensor, 1, 0)


def group_pass(query_blocks, key_blocks, value_blocks, decay_blocks, initial):
    inner = jnp.cumsum(decay_blocks, axis=2)
    ending = inner[:, :, -1:, :]
    query_in = query_blocks * jnp.exp(inner)
    key_in = key_blocks * jnp.exp(-inner)
    key_end = key_blocks * jnp.exp(ending - inner)
    length = query_blocks.shape[2]
    causal = jnp.tril(jnp.ones((length, length), jnp.float32))
    scores = jnp.einsum("hnck,hnsk->hncs", query_in, key_in, precision=TOP_PRECISION) * causal
    within = jnp.einsum("hncs,hnsv->hncv", scores, value_blocks, precision=TOP_PRECISION)

    def advance(carried_state, sequence_segments):
        query_segment, key_segment, value_segment, fading_factor = sequence_segments
        block_result = jnp.einsum(
            "waq,wqo->wao", query_segment, carried_state, precision=TOP_PRECISION
        )
        carried_state = fading_factor[:, 0, :, None] * carried_state + jnp.einsum(
            "fjb,fjq->fbq", key_segment, value_segment, precision=TOP_PRECISION
        )
        return (carried_state, block_result)

    final, across_pieces = lax.scan(
        advance,
        initial,
        (to_front(query_in), to_front(key_end), to_front(value_blocks), to_front(jnp.exp(ending))),
    )
    return (within + to_front(across_pieces), final)


def post_gate(mixer, outgate, head_gain):
    tokens_here = mixer.shape[0]
    per_head = mixer.reshape(tokens_here, H, VALUE_WIDTH)
    normed = rms_norm(per_head, head_gain).reshape(tokens_here, H * VALUE_WIDTH)
    return normed * outgate * jax.nn.sigmoid(outgate)


def local_pass(query, keys, values, decay_logit):
    log_decay = jax.nn.log_sigmoid(decay_logit) / GATE_NORM
    query_blocks = split_into_heads(query, DK)
    decay_blocks = split_into_heads(log_decay, DK)
    zero_state = jnp.zeros((H, DK, VALUE_WIDTH), jnp.float32)
    local_out, local_state = group_pass(
        query_blocks,
        split_into_heads(keys, DK),
        split_into_heads(values, VALUE_WIDTH),
        decay_blocks,
        zero_state,
    )
    layout = decay_blocks.shape
    cumulative = jnp.cumsum(
        decay_blocks.reshape(layout[0], layout[1] * layout[2], layout[3]), axis=1
    ).reshape(layout)
    log_fading = cumulative[:, -1, -1, :]
    query_fading = query_blocks * jnp.exp(cumulative)
    return (query_fading, log_fading, local_out, local_state)


def finish(sequence_segments, incoming_state):
    query_fading, log_fading, local_out, local_state = sequence_segments
    across_pieces = jnp.einsum(
        "qwxg,qgf->qwxf", query_fading, incoming_state, precision=TOP_PRECISION
    )
    return (
        from_heads(local_out + across_pieces),
        jnp.exp(log_fading)[:, :, None] * incoming_state + local_state,
    )


def local(
    block_input,
    cotangent,
    attn_gain,
    w_query,
    w_key,
    w_value,
    w_outgate,
    w_decay_down,
    w_decay_up,
    decay_bias,
    head_gain,
    w_out,
    mlp_gain,
    w_gate,
    w_up,
    w_down,
):
    count = lax.axis_size("seq")
    rows = w_query.shape[0]
    key_width, value_width, rank = (w_query.shape[1], w_value.shape[1], w_decay_down.shape[1])
    hidden = w_gate.shape[1]
    small_shapes = (w_decay_up.shape, attn_gain.shape, mlp_gain.shape, decay_bias.shape, head_gain.shape)
    first = jnp.concatenate(
        [
            w_query,
            w_key,
            w_value,
            w_outgate,
            jnp.pad(w_decay_down, ((0, 0), (0, LANES - rank))),
            pack_small((w_decay_up, attn_gain, mlp_gain, decay_bias, head_gain), rows),
            w_out,
        ],
        axis=1,
    )
    first = lax.all_gather(first, "seq", axis=0, tiled=True)
    levels = count // PLANE
    planes, columns = (plane_groups(count), level_groups(count))
    units = levels * w_down.shape[0]
    padded = -(-units // LANES) * LANES
    gate_up = jnp.concatenate([to_units(w_gate, levels, padded), to_units(w_up, levels, padded)], axis=2)
    gate_up = lax.all_to_all(gate_up, "seq", 0, 0, axis_index_groups=planes)
    gate_up = gate_up.reshape(PLANE * rows, 2 * padded)
    gate_up = lax.all_gather(gate_up, "seq", axis=0, tiled=True, axis_index_groups=columns)
    down = lax.all_gather(w_down, "seq", axis=0, tiled=True, axis_index_groups=columns)
    down = jnp.pad(down, ((0, padded - units), (0, 0)))
    cot_in, first = lax.optimization_barrier((cotangent.astype(jnp.bfloat16), first))
    cot_plane = plane_gather(cot_in)
    widths = (key_width, key_width, value_width, value_width)
    wide = 2 * key_width + 2 * value_width
    projection = first[:, : wide + LANES]
    small = first[:, wide + LANES : wide + 2 * LANES].reshape(count, rows * LANES)
    up_pieces, attn_full, mlp_full_gain, bias_full, head_full = unpack_small(small, small_shapes)
    decay_up_full = up_pieces.transpose(1, 0, 2).reshape(rank, key_width)
    attn_full, mlp_full_gain, bias_full, head_full = (
        piece.reshape(-1).astype(jnp.float32) for piece in (attn_full, mlp_full_gain, bias_full, head_full)
    )
    out_full = first[:, wide + 2 * LANES :]
    scaling = DK ** (-0.5)
    normed, norm_back = jax.vjp(rms_norm, block_input, attn_full)
    normed_in = normed.astype(jnp.bfloat16)
    query, keys, values, outgate, low_rank = column_slices(
        matmul(normed_in, projection), widths + (rank,)
    )
    query = query * scaling
    low_rank = low_rank.astype(jnp.bfloat16)
    decay_logit = matmul(low_rank, decay_up_full) + bias_full
    sequence_segments, local_back = jax.vjp(local_pass, query, keys, values, decay_logit)
    chunk = key_width // count
    state = sequence_segments[3].reshape(key_width, VALUE_WIDTH).astype(jnp.bfloat16)
    log_pieces = three_pieces(sequence_segments[1].reshape(-1)).T
    log_pieces = jnp.pad(log_pieces, ((0, 0), (0, LANES - 3)))
    arrived = exchange(
        jnp.concatenate([state, log_pieces], axis=1).reshape(count, chunk, VALUE_WIDTH + LANES)
    )
    logs = arrived[:, :, VALUE_WIDTH:]
    before = exchange(scan_devices(prefix_body, arrived[:, :, :VALUE_WIDTH], logs))
    incoming_state = before.reshape(H, DK, VALUE_WIDTH).astype(jnp.float32)
    mixer, state_after = finish(sequence_segments, incoming_state)
    gated_full, post_back = jax.vjp(post_gate, mixer, outgate, head_full)
    gated = gated_full.astype(jnp.bfloat16)
    hidden_state = block_input + matmul(gated, out_full)
    mlp_full, mlp_back = jax.vjp(rms_norm, hidden_state, mlp_full_gain)
    mlp_normed = mlp_full.astype(jnp.bfloat16)
    mlp_plane = plane_gather(mlp_normed)
    gate_pre, up_pre = column_slices(matmul(mlp_plane, gate_up), (padded, padded))
    activ_full, activ_back = jax.vjp(swiglu, gate_pre, up_pre)
    activ = activ_full.astype(jnp.bfloat16)
    d_activ = times_back(cot_plane, down)
    d_gate_full, d_up_full = activ_back(d_activ)
    d_gate_up = jnp.concatenate(
        [d_gate_full.astype(jnp.bfloat16), d_up_full.astype(jnp.bfloat16)], axis=1
    )
    d_mlp_normed = plane_scatter(times_back(d_gate_up, gate_up))
    activ_late, d_mlp_normed = lax.optimization_barrier((activ, d_mlp_normed))
    block_output = hidden_state + plane_scatter(matmul(activ_late, down))

    def level_sum(partial):
        return lax.psum_scatter(
            partial.astype(jnp.bfloat16),
            "seq",
            scatter_dimension=0,
            tiled=True,
            axis_index_groups=columns,
        )

    sum_down = level_sum(outer_sum(activ, cot_plane)[:units]).astype(jnp.float32)
    sum_gate_up = level_sum(outer_sum(mlp_plane, d_gate_up)).reshape(PLANE, rows, 2 * padded)
    sum_gate_up = lax.all_to_all(sum_gate_up, "seq", 0, 0, axis_index_groups=planes)
    sum_gate_up = sum_gate_up.astype(jnp.float32)
    sum_gate = from_units(sum_gate_up[:, :, :padded], levels, hidden)
    sum_up_proj = from_units(sum_gate_up[:, :, padded:], levels, hidden)
    d_hidden_norm, grad_mlp_gain = mlp_back(d_mlp_normed)
    d_hidden = cotangent + d_hidden_norm
    d_hidden_in = d_hidden.astype(jnp.bfloat16)
    d_gated = times_back(d_hidden_in, out_full)
    mixer_gradient, d_outgate, grad_head_gain = post_back(d_gated)
    state_gradient = jnp.einsum(
        "ryfm,ryfj->rmj",
        sequence_segments[0],
        split_into_heads(mixer_gradient, VALUE_WIDTH),
        precision=TOP_PRECISION,
    )
    arrived_back = exchange(
        state_gradient.reshape(count, chunk, VALUE_WIDTH).astype(jnp.bfloat16)
    )
    after = exchange(scan_devices(suffix_body, arrived_back, logs))
    after = after.reshape(H, DK, VALUE_WIDTH).astype(jnp.float32)
    finish_value, finish_back = jax.vjp(finish, sequence_segments, incoming_state)
    d_pieces, d_incoming = finish_back((mixer_gradient, after))
    d_query, d_keys, d_values, d_logit = local_back(d_pieces)
    grad_decay_bias = jnp.sum(d_logit, axis=0)
    d_logit_in = d_logit.astype(jnp.bfloat16)
    grad_decay_up = outer_sum(low_rank, d_logit_in)
    d_low = times_back(d_logit_in, decay_up_full).astype(jnp.bfloat16)
    d_first = jnp.concatenate(
        [
            (d_query * scaling).astype(jnp.bfloat16),
            d_keys.astype(jnp.bfloat16),
            d_values.astype(jnp.bfloat16),
            d_outgate.astype(jnp.bfloat16),
            jnp.pad(d_low, ((0, 0), (0, LANES - rank))),
        ],
        axis=1,
    )
    d_normed = times_back(d_first, projection)
    d_input_norm, grad_attn_gain = norm_back(d_normed)
    input_grad = d_hidden + d_input_norm

    small_sums = pack_small_sums(
        (
            grad_decay_up.reshape(rank, count, -1).transpose(1, 0, 2),
            grad_attn_gain,
            grad_mlp_gain,
            grad_decay_bias,
            grad_head_gain,
        ),
        count,
    )
    small_sums = jnp.sum(exchange(small_sums), axis=0)
    order = neighbour_ring(count)
    chips = tuple(device // 2 for device in order[::2])
    rings = [[2 * chip + core for chip in chips] for core in range(2)]
    parity = lax.axis_index("seq") % 2
    normed_pair = own_columns(with_partner(normed_in), chips, parity, rows)
    gated_pair = own_columns(with_partner(gated), chips, parity, rows)
    width = wide + LANES + w_out.shape[1]
    sums = grad_into(gated_pair, with_partner(d_hidden_in), None, width, wide + LANES, LANES)
    sums = grad_into(normed_pair, with_partner(d_first), sums, width, 0, 640)
    sums = lax.psum_scatter(
        sums, "seq", scatter_dimension=0, tiled=True, axis_index_groups=rings
    ).astype(jnp.float32)
    sum_first, sum_out = column_slices(sums, (wide + LANES, w_out.shape[1]))
    sum_query, sum_key, sum_value, sum_outgate, sum_decay_down = column_slices(
        sum_first, widths + (rank,)
    )
    sum_up, sum_attn, sum_mlp, sum_bias, sum_head = unpack_small(
        small_sums, small_shapes
    )
    return (
        block_output,
        input_grad,
        sum_attn,
        sum_query,
        sum_key,
        sum_value,
        sum_outgate,
        sum_decay_down,
        sum_up,
        sum_bias,
        sum_head,
        sum_out,
        sum_mlp,
        sum_gate,
        sum_up_proj,
        sum_down,
    )


def solution(mesh):
    return jax.shard_map(
        local,
        mesh=mesh,
        in_specs=(
            P("seq", None),
            P("seq", None),
            P("seq"),
            P("seq", None),
            P("seq", None),
            P("seq", None),
            P("seq", None),
            P("seq", None),
            P(None, "seq"),
            P("seq"),
            P("seq"),
            P("seq", None),
            P("seq"),
            P("seq", None),
            P("seq", None),
            P("seq", None),
        ),
        out_specs=(
            P("seq", None),
            P("seq", None),
            P("seq"),
            P("seq", None),
            P("seq", None),
            P("seq", None),
            P("seq", None),
            P("seq", None),
            P(None, "seq"),
            P("seq"),
            P("seq"),
            P("seq", None),
            P("seq"),
            P("seq", None),
            P("seq", None),
            P("seq", None),
        ),
        check_vma=False,
    )
```

```python
import jax
import jax.numpy as jnp
from jax import lax
from jax.experimental import pallas as pl
from jax.experimental.pallas import tpu as pltpu
from jax.sharding import PartitionSpec as P

H = 4
DK = 128
VALUE_WIDTH = 256
GROUP = 64


EPS = 1e-05
GATE_NORM = 16.0
TOP_PRECISION = lax.Precision.HIGHEST


LANES = 128


def pack_small(pieces):
    flat = jnp.concatenate([piece.reshape(-1) for piece in pieces])
    return jnp.pad(flat, (0, -flat.shape[0] % LANES))


def pack_small_sums(pieces, devices):
    flat = jnp.concatenate([piece.reshape(devices, -1) for piece in pieces], axis=1)
    return jnp.pad(flat, ((0, 0), (0, -flat.shape[1] % LANES)))


def unpack_small(flat, shapes):
    pieces, at = [], 0
    for shape in shapes:
        size = 1
        for extent in shape:
            size *= extent
        pieces.append(flat[..., at : at + size].reshape(flat.shape[:-1] + shape))
        at += size
    return pieces


def column_slices(array, widths):
    pieces, at = [], 0
    for width in widths:
        pieces.append(array[:, at : at + width])
        at += width
    return pieces


def neighbour_ring(count):
    if count % 8:
        return tuple(range(count))
    levels, order = count // 8, []
    for column, chip in enumerate((0, 1, 3, 2)):
        climb = range(levels) if column % 2 == 0 else range(levels - 1, -1, -1)
        for level in climb:
            order += [8 * level + 2 * chip, 8 * level + 2 * chip + 1]
    return tuple(order)


def in_vmem():
    return pl.BlockSpec(memory_space=pltpu.VMEM)


def prefix_body(states, logs, out):
    count = states.shape[0]
    carried = jnp.zeros(states.shape[1:], jnp.float32)
    for device in range(count):
        out[device] = carried.astype(out.dtype)
        fading = jnp.exp(logs[device].astype(jnp.float32).sum(axis=-1, keepdims=True))
        carried = fading * carried + states[device].astype(jnp.float32)


def suffix_body(states, logs, out):
    count = states.shape[0]
    carried = jnp.zeros(states.shape[1:], jnp.float32)
    for device in range(count - 1, -1, -1):
        out[device] = carried.astype(out.dtype)
        fading = jnp.exp(logs[device].astype(jnp.float32).sum(axis=-1, keepdims=True))
        carried = fading * carried + states[device].astype(jnp.float32)


def scan_devices(body, states, logs):
    return pl.pallas_call(
        body,
        out_shape=jax.ShapeDtypeStruct(states.shape, jnp.bfloat16),
        in_specs=[in_vmem(), in_vmem()],
        out_specs=in_vmem(),
    )(states, logs)


def exchange(array):
    return lax.all_to_all(array, "seq", 0, 0)


PLANE = 8
OFFSETS = (0, 2, 4, 6)


def plane_groups(count):
    return [list(range(start, start + PLANE)) for start in range(0, count, PLANE)]


def level_groups(count):
    return [list(range(place, count, PLANE)) for place in range(PLANE)]


def swapped(array, offset):
    count = lax.axis_size("seq")
    return lax.ppermute(array, "seq", [(device, device ^ offset) for device in range(count)])


def plane_gather(array):
    same = [array] + [swapped(array, offset) for offset in OFFSETS[1:]]
    return jnp.concatenate(same + [swapped(part, 1) for part in same], axis=0)


def plane_scatter(partial):
    half = partial.shape[0] // 2
    rows = half // len(OFFSETS)
    joined = partial[:half] + swapped(partial[half:].astype(jnp.bfloat16), 1).astype(jnp.float32)
    total = joined[:rows]
    for place, offset in enumerate(OFFSETS[1:], 1):
        piece = joined[place * rows : (place + 1) * rows].astype(jnp.bfloat16)
        total = total + swapped(piece, offset).astype(jnp.float32)
    return total


def to_units(weight, levels, padded):
    rows, hidden = weight.shape
    width = hidden // (levels * PLANE)
    parts = weight.reshape(rows, levels, PLANE, width).transpose(2, 0, 1, 3)
    parts = parts.reshape(PLANE, rows, levels * width)
    return jnp.pad(parts, ((0, 0), (0, 0), (0, padded - levels * width)))


def from_units(parts, levels, hidden):
    rows = parts.shape[1]
    width = hidden // (levels * PLANE)
    parts = parts[:, :, : levels * width].reshape(PLANE, rows, levels, width)
    return parts.transpose(1, 2, 0, 3).reshape(rows, hidden)


def grad_body(left, own, other, *rest):
    out = rest[-1]
    tokens = own.shape[0]
    total = outer_sum(left[:tokens, :], own[...]) + outer_sum(left[tokens:, :], other[...])
    out[...] = total.astype(out.dtype)


def grad_into(left, right, buffer, total, start, block):
    tokens, height = left.shape
    first = start // block
    operands = [left, right, swapped(right, 1)]
    specs = [
        pl.BlockSpec((tokens, height), lambda j: (0, 0)),
        pl.BlockSpec((tokens // 2, block), lambda j: (0, j)),
        pl.BlockSpec((tokens // 2, block), lambda j: (0, j)),
    ]
    aliases = {}
    if buffer is not None:
        aliases = {len(operands): 0}
        operands.append(buffer)
        specs.append(pl.BlockSpec(memory_space=pl.ANY))
    return pl.pallas_call(
        grad_body,
        grid=(pl.cdiv(right.shape[1], block),),
        in_specs=specs,
        out_specs=pl.BlockSpec((height, block), lambda j: (0, j + first)),
        out_shape=jax.ShapeDtypeStruct((height, total), jnp.bfloat16),
        input_output_aliases=aliases,
    )(*operands)


def with_partner(array):
    return jnp.concatenate([array, swapped(array, 1)], axis=0)


def own_columns(array, chips, parity, rows):
    width = array.shape[1]
    column = jnp.arange(width // 2)
    place = jnp.asarray(chips, jnp.int32)[column // rows]
    source = (2 * place + parity) * rows + column % rows
    pick = jnp.arange(width)[:, None] == source[None, :]
    return jnp.dot(array, pick.astype(array.dtype), preferred_element_type=array.dtype)


def matmul(left_side, right_side):
    return jnp.dot(left_side, right_side, preferred_element_type=jnp.float32)


def times_back(left_side, right_side):
    return lax.dot_general(
        left_side, right_side, (((1,), (1,)), ((), ())), preferred_element_type=jnp.float32
    )


def outer_sum(left_side, right_side):
    return lax.dot_general(
        left_side, right_side, (((0,), (0,)), ((), ())), preferred_element_type=jnp.float32
    )


def rms_norm(matrix, gain):
    scaling = lax.rsqrt(jnp.mean(matrix * matrix, axis=-1, keepdims=True) + EPS)
    return matrix * scaling * gain


def swiglu(gate_pre, up_pre):
    return jax.nn.silu(gate_pre) * up_pre


def sized(left, right, contract, precision=TOP_PRECISION):
    return lax.dot_general(
        left, right, (contract, ((), ())), precision=precision, preferred_element_type=jnp.float32
    )


ROWS_BY_ROWS = ((0,), (0,))
COLUMNS_BY_COLUMNS = ((1,), (1,))
PLAIN = ((1,), (0,))


def triangle(size, lower=True):
    row = lax.broadcasted_iota(jnp.int32, (size, size), 0)
    column = lax.broadcasted_iota(jnp.int32, (size, size), 1)
    return (row >= column if lower else row <= column).astype(jnp.float32)


def log_decay_of(logit):
    return (jnp.minimum(logit, 0.0) - jnp.log1p(jnp.exp(-jnp.abs(logit)))) / GATE_NORM


def state_body(key, value, low, up, bias, logit_out, out):
    tokens, width = key.shape
    logit = sized(low[...].astype(jnp.bfloat16), up[...], PLAIN, None) + bias[...]
    logit_out[...] = logit
    log_decay = log_decay_of(logit)
    later = 1.0 - triangle(tokens)
    remaining = sized(later, log_decay, PLAIN)
    state = sized(key[...] * jnp.exp(remaining), value[...], ROWS_BY_ROWS)
    total = sized(log_decay, jnp.ones((tokens, LANES), jnp.float32), ROWS_BY_ROWS)
    high = total.astype(jnp.bfloat16).astype(jnp.float32)
    middle = (total - high).astype(jnp.bfloat16).astype(jnp.float32)
    lane = lax.broadcasted_iota(jnp.int32, (width, LANES), 1)
    pieces = jnp.where(lane == 0, high, jnp.where(lane == 1, middle, total - high - middle))
    out[:, : state.shape[1]] = state.astype(out.dtype)
    out[:, state.shape[1] :] = jnp.where(lane < 3, pieces, 0.0).astype(out.dtype)


def block_terms(query, key, log_decay):
    inner = sized(triangle(GROUP), log_decay, PLAIN)
    ending = inner[GROUP - 1 : GROUP, :]
    rising, falling = jnp.exp(inner), jnp.exp(-inner)
    fading = jnp.exp(ending - inner)
    return rising, falling, fading, query * rising, key * falling, key * fading


def ending_columns(log_decay, width):
    return jnp.exp(sized(log_decay, jnp.ones((log_decay.shape[0], width), jnp.float32), ROWS_BY_ROWS))


def output_body(query, key, value, logit, outgate, gain, entering, mixer_out, gated_out):
    state = entering[...].astype(jnp.float32)
    causal = triangle(GROUP)
    count = query.shape[0] // GROUP
    for block in range(count):
        at = slice(block * GROUP, (block + 1) * GROUP)
        log_decay = log_decay_of(logit[at, :])
        values = value[at, :]
        _, _, _, query_in, key_in, key_end = block_terms(
            query[at, :] * DK ** (-0.5), key[at, :], log_decay
        )
        scores = sized(query_in, key_in, COLUMNS_BY_COLUMNS) * causal
        mixer = sized(scores, values, PLAIN) + sized(query_in, state, PLAIN)
        if block < count - 1:
            state = ending_columns(log_decay, state.shape[1]) * state + sized(
                key_end, values, ROWS_BY_ROWS
            )
        mixer_out[at, :] = mixer
        scale = lax.rsqrt(jnp.mean(mixer * mixer, axis=-1, keepdims=True) + EPS)
        gate = outgate[at, :]
        gated_out[at, :] = (mixer * scale * gain[...] * gate * jax.nn.sigmoid(gate)).astype(
            gated_out.dtype
        )


def gate_back_body(
    d_gated, mixer, outgate, gain, query, logit, d_mixer_out, d_gate_out, gain_out, state_out
):
    tokens = query.shape[0]
    scale = lax.rsqrt(jnp.mean(mixer[...] * mixer[...], axis=-1, keepdims=True) + EPS)
    unit = mixer[...] * scale
    sigmoid = jax.nn.sigmoid(outgate[...])
    gradient = d_gated[...] * outgate[...] * sigmoid
    inward = gradient * gain[...]
    d_mixer = scale * (inward - unit * jnp.mean(inward * unit, axis=-1, keepdims=True))
    d_mixer_out[...] = d_mixer
    d_gate = d_gated[...] * unit * gain[...] * sigmoid * (1.0 + outgate[...] * (1.0 - sigmoid))
    d_gate_out[...] = d_gate.astype(d_gate_out.dtype)

    @pl.when(pl.program_id(0) == 0)
    def _():
        gain_out[...] = jnp.zeros(gain_out.shape, jnp.float32)

    gain_out[...] += jnp.sum(gradient * unit, axis=0, keepdims=True)
    cumulative = sized(triangle(tokens), log_decay_of(logit[...]), PLAIN)
    state_out[...] = sized(
        query[...] * (DK ** (-0.5)) * jnp.exp(cumulative), d_mixer, ROWS_BY_ROWS
    ).astype(state_out.dtype)


def mixer_back_body(
    query, key, value, logit, d_mixer, entering, leaving, d_gate, up, out, d_logit_out, bias_out, low
):
    head = pl.program_id(0)
    heads = pl.num_programs(0)
    width, value_width = key.shape[1], value.shape[1]
    count = query.shape[0] // GROUP
    causal, upper = triangle(GROUP), triangle(GROUP, lower=False)
    ones = jnp.ones((8, value_width), jnp.float32)
    state, blocks = entering[...].astype(jnp.float32), []
    for block in range(count):
        at = slice(block * GROUP, (block + 1) * GROUP)
        log_decay = log_decay_of(logit[at, :])
        terms = block_terms(query[at, :] * DK ** (-0.5), key[at, :], log_decay)
        factor = ending_columns(log_decay, value_width)
        blocks.append((at, terms, factor, state))
        if block < count - 1:
            state = factor * state + sized(terms[5], value[at, :], ROWS_BY_ROWS)
    d_state = leaving[...].astype(jnp.float32)
    bias_sum = jnp.zeros((1, width), jnp.float32)
    for at, terms, factor, state in reversed(blocks):
        rising, falling, fading, query_in, key_in, key_end = terms
        values, d_out = value[at, :], d_mixer[at, :]
        scores = sized(query_in, key_in, COLUMNS_BY_COLUMNS) * causal
        d_scores = sized(d_out, values, COLUMNS_BY_COLUMNS) * causal
        d_query_in = sized(d_scores, key_in, PLAIN) + sized(d_out, state, COLUMNS_BY_COLUMNS)
        d_key_in = sized(d_scores, query_in, ROWS_BY_ROWS)
        d_values = sized(scores, d_out, ROWS_BY_ROWS) + sized(key_end, d_state, PLAIN)
        d_key_end = sized(values, d_state, COLUMNS_BY_COLUMNS)
        d_ending = sized(ones, d_state * factor * state, COLUMNS_BY_COLUMNS)[0:1, :]
        end_part = d_key_end * key_end
        d_ending = d_ending + jnp.sum(end_part, axis=0, keepdims=True)
        d_inner = d_query_in * query_in - d_key_in * key_in - end_part
        d_log_decay = sized(upper, d_inner, PLAIN) + d_ending
        d_logit = d_log_decay * jax.nn.sigmoid(-logit[at, :]) / GATE_NORM
        bias_sum = bias_sum + jnp.sum(d_logit, axis=0, keepdims=True)
        d_logit_in = d_logit.astype(jnp.bfloat16)
        d_logit_out[at, :] = d_logit_in
        d_low = sized(d_logit_in, up[...], COLUMNS_BY_COLUMNS, None)
        d_low = jnp.where(head == 0, d_low, d_low + low[at, :])
        low[at, :] = d_low
        d_state = factor * d_state + sized(query_in, d_out, ROWS_BY_ROWS)
        at_query = pl.multiple_of(head * width, width)
        at_key = pl.multiple_of((heads + head) * width, width)
        at_value = pl.multiple_of(2 * heads * width + head * value_width, value_width)
        at_gate = pl.multiple_of(2 * heads * width + (heads + head) * value_width, value_width)
        at_low = 2 * heads * (width + value_width)
        out[at, pl.ds(at_query, width)] = (DK ** (-0.5) * d_query_in * rising).astype(out.dtype)
        out[at, pl.ds(at_key, width)] = (d_key_in * falling + d_key_end * fading).astype(out.dtype)
        out[at, pl.ds(at_value, value_width)] = d_values.astype(out.dtype)
        out[at, pl.ds(at_gate, value_width)] = d_gate[at, :]
        out[at, at_low:] = d_low.astype(out.dtype)
    bias_out[...] = bias_sum


def per_head(rows, columns, offset=0):
    return pl.BlockSpec((rows, columns), lambda head: (0, head + offset))


def per_head_rows(rows, columns):
    return pl.BlockSpec((rows, columns), lambda head: (head, 0))


def whole_at(rows, columns, place):
    return pl.BlockSpec((rows, columns), lambda head: (0, place))


def whole(rows, columns):
    return pl.BlockSpec((rows, columns), lambda head: (0, 0))


def local(
    block_input,
    cotangent,
    attn_gain,
    w_query,
    w_key,
    w_value,
    w_outgate,
    w_decay_down,
    w_decay_up,
    decay_bias,
    head_gain,
    w_out,
    mlp_gain,
    w_gate,
    w_up,
    w_down,
):
    count = lax.axis_size("seq")
    rows = w_query.shape[0]
    key_width, value_width, rank = (w_query.shape[1], w_value.shape[1], w_decay_down.shape[1])
    hidden = w_gate.shape[1]
    small_shapes = (w_decay_up.shape, attn_gain.shape, mlp_gain.shape, decay_bias.shape, head_gain.shape)
    first = jnp.concatenate(
        [
            w_query,
            w_key,
            w_value,
            w_outgate,
            jnp.pad(w_decay_down, ((0, 0), (0, LANES - rank))),
            w_out,
        ],
        axis=1,
    )
    small = pack_small((w_decay_up, attn_gain, mlp_gain, decay_bias, head_gain))
    small = exchange(jnp.broadcast_to(small, (count, 1) + small.shape)).reshape(count, -1)
    first = lax.all_gather(first, "seq", axis=0, tiled=True)
    levels = count // PLANE
    planes, columns = (plane_groups(count), level_groups(count))
    units = levels * w_down.shape[0]
    padded = -(-units // LANES) * LANES
    gate_up = jnp.concatenate([to_units(w_gate, levels, padded), to_units(w_up, levels, padded)], axis=2)
    gate_up = lax.all_to_all(gate_up, "seq", 0, 0, axis_index_groups=planes)
    gate_up = gate_up.reshape(PLANE * rows, 2 * padded)
    gate_up = lax.all_gather(gate_up, "seq", axis=0, tiled=True, axis_index_groups=columns)
    down = lax.all_gather(w_down, "seq", axis=0, tiled=True, axis_index_groups=columns)
    down = jnp.pad(down, ((0, padded - units), (0, 0)))
    cot_in, first = lax.optimization_barrier((cotangent.astype(jnp.bfloat16), first))
    cot_plane = plane_gather(cot_in)
    widths = (key_width, key_width, value_width, value_width)
    wide = 2 * key_width + 2 * value_width
    projection = first[:, : wide + LANES]
    up_pieces, attn_full, mlp_full_gain, bias_full, head_full = unpack_small(small, small_shapes)
    decay_up_full = up_pieces.transpose(1, 0, 2).reshape(rank, key_width)
    attn_full, mlp_full_gain, bias_full, head_full = (
        piece.reshape(-1).astype(jnp.float32) for piece in (attn_full, mlp_full_gain, bias_full, head_full)
    )
    out_full = first[:, wide + LANES :]
    scaling = DK ** (-0.5)
    normed, norm_back = jax.vjp(rms_norm, block_input, attn_full)
    normed_in = normed.astype(jnp.bfloat16)
    wide_out = matmul(normed_in, projection)
    tokens = wide_out.shape[0]
    up_rows = jnp.pad(decay_up_full, ((0, LANES - rank), (0, 0)))
    value_at = 2 * key_width // VALUE_WIDTH
    query_spec, key_spec = per_head(tokens, DK), per_head(tokens, DK, H)
    value_spec = per_head(tokens, VALUE_WIDTH, value_at)
    gate_spec = per_head(tokens, VALUE_WIDTH, value_at + H)
    low_spec = whole_at(tokens, LANES, wide // LANES)
    up_spec = per_head(LANES, DK)
    head_values, head_keys = per_head(tokens, VALUE_WIDTH), per_head(tokens, DK)
    state_spec = per_head_rows(DK, VALUE_WIDTH)
    gain_spec = whole(1, VALUE_WIDTH)
    gain_row = head_full[None, :]
    chunk = key_width // count
    decay_logit, outgoing = pl.pallas_call(
        state_body,
        grid=(H,),
        in_specs=[key_spec, value_spec, low_spec, up_spec, per_head(1, DK)],
        out_specs=[head_keys, per_head_rows(DK, VALUE_WIDTH + LANES)],
        out_shape=[
            jax.ShapeDtypeStruct((tokens, key_width), jnp.float32),
            jax.ShapeDtypeStruct((key_width, VALUE_WIDTH + LANES), jnp.bfloat16),
        ],
    )(wide_out, wide_out, wide_out, up_rows, bias_full[None, :])
    arrived = exchange(outgoing.reshape(count, chunk, VALUE_WIDTH + LANES))
    logs = arrived[:, :, VALUE_WIDTH:]
    before = exchange(scan_devices(prefix_body, arrived[:, :, :VALUE_WIDTH], logs))
    before = before.reshape(key_width, VALUE_WIDTH)
    mixer, gated = pl.pallas_call(
        output_body,
        grid=(H,),
        in_specs=[query_spec, key_spec, value_spec, head_keys, gate_spec, gain_spec, state_spec],
        out_specs=[head_values, head_values],
        out_shape=[
            jax.ShapeDtypeStruct((tokens, value_width), jnp.float32),
            jax.ShapeDtypeStruct((tokens, value_width), jnp.bfloat16),
        ],
    )(wide_out, wide_out, wide_out, decay_logit, wide_out, gain_row, before)
    hidden_state = block_input + matmul(gated, out_full)
    mlp_full, mlp_back = jax.vjp(rms_norm, hidden_state, mlp_full_gain)
    mlp_normed = mlp_full.astype(jnp.bfloat16)
    mlp_plane = plane_gather(mlp_normed)
    gate_pre, up_pre = column_slices(matmul(mlp_plane, gate_up), (padded, padded))
    activ_full, activ_back = jax.vjp(swiglu, gate_pre, up_pre)
    activ = activ_full.astype(jnp.bfloat16)
    d_activ = times_back(cot_plane, down)
    d_gate_full, d_up_full = activ_back(d_activ)
    d_gate_up = jnp.concatenate(
        [d_gate_full.astype(jnp.bfloat16), d_up_full.astype(jnp.bfloat16)], axis=1
    )
    d_mlp_normed = plane_scatter(times_back(d_gate_up, gate_up))

    def level_sum(partial):
        return lax.psum_scatter(
            partial.astype(jnp.bfloat16),
            "seq",
            scatter_dimension=0,
            tiled=True,
            axis_index_groups=columns,
        )

    sum_down = level_sum(outer_sum(activ, cot_plane)[:units]).astype(jnp.float32)
    sum_gate_up = level_sum(outer_sum(mlp_plane, d_gate_up)).reshape(PLANE, rows, 2 * padded)
    sum_gate_up = lax.all_to_all(sum_gate_up, "seq", 0, 0, axis_index_groups=planes)
    sum_gate_up = sum_gate_up.astype(jnp.float32)
    sum_gate = from_units(sum_gate_up[:, :, :padded], levels, hidden)
    sum_up_proj = from_units(sum_gate_up[:, :, padded:], levels, hidden)
    d_hidden_norm, grad_mlp_gain = mlp_back(d_mlp_normed)
    d_hidden = cotangent + d_hidden_norm
    d_hidden_in = d_hidden.astype(jnp.bfloat16)
    d_gated = times_back(d_hidden_in, out_full)
    mixer_gradient, d_outgate, grad_head_gain, state_gradient = pl.pallas_call(
        gate_back_body,
        grid=(H,),
        in_specs=[head_values, head_values, gate_spec, gain_spec, query_spec, head_keys],
        out_specs=[head_values, head_values, gain_spec, state_spec],
        out_shape=[
            jax.ShapeDtypeStruct((tokens, value_width), jnp.float32),
            jax.ShapeDtypeStruct((tokens, value_width), jnp.bfloat16),
            jax.ShapeDtypeStruct((1, VALUE_WIDTH), jnp.float32),
            jax.ShapeDtypeStruct((key_width, VALUE_WIDTH), jnp.bfloat16),
        ],
    )(d_gated, mixer, wide_out, gain_row, wide_out, decay_logit)
    arrived_back = exchange(state_gradient.reshape(count, chunk, VALUE_WIDTH))
    after = exchange(scan_devices(suffix_body, arrived_back, logs))
    activ_late, after = lax.optimization_barrier((activ, after))
    block_output = hidden_state + plane_scatter(matmul(activ_late, down))
    after = after.reshape(key_width, VALUE_WIDTH)
    d_first, d_logit_in, grad_decay_bias = pl.pallas_call(
        mixer_back_body,
        grid=(H,),
        in_specs=[
            query_spec,
            key_spec,
            value_spec,
            head_keys,
            head_values,
            state_spec,
            state_spec,
            head_values,
            up_spec,
        ],
        out_specs=[whole(tokens, wide + LANES), head_keys, per_head(1, DK)],
        out_shape=[
            jax.ShapeDtypeStruct((tokens, wide + LANES), jnp.bfloat16),
            jax.ShapeDtypeStruct((tokens, key_width), jnp.bfloat16),
            jax.ShapeDtypeStruct((1, key_width), jnp.float32),
        ],
        scratch_shapes=[pltpu.VMEM((tokens, LANES), jnp.float32)],
    )(
        wide_out,
        wide_out,
        wide_out,
        decay_logit,
        mixer_gradient,
        before,
        after,
        d_outgate,
        up_rows,
    )
    low_rank = wide_out[:, wide : wide + rank].astype(jnp.bfloat16)
    grad_decay_up = outer_sum(low_rank, d_logit_in)
    d_normed = times_back(d_first, projection)
    d_input_norm, grad_attn_gain = norm_back(d_normed)
    input_grad = d_hidden + d_input_norm

    small_sums = pack_small_sums(
        (
            grad_decay_up.reshape(rank, count, -1).transpose(1, 0, 2),
            grad_attn_gain,
            grad_mlp_gain,
            grad_decay_bias,
            grad_head_gain.reshape(-1),
        ),
        count,
    )
    small_sums = jnp.sum(exchange(small_sums), axis=0)
    order = neighbour_ring(count)
    chips = tuple(device // 2 for device in order[::2])
    rings = [[2 * chip + core for chip in chips] for core in range(2)]
    parity = lax.axis_index("seq") % 2
    normed_pair = own_columns(with_partner(normed_in), chips, parity, rows)
    gated_pair = own_columns(with_partner(gated), chips, parity, rows)
    width = wide + LANES + w_out.shape[1]
    sums = grad_into(gated_pair, d_hidden_in, None, width, wide + LANES, LANES)
    sums = grad_into(normed_pair, d_first, sums, width, 0, 640)
    sums = lax.psum_scatter(
        sums, "seq", scatter_dimension=0, tiled=True, axis_index_groups=rings
    ).astype(jnp.float32)
    sum_first, sum_out = column_slices(sums, (wide + LANES, w_out.shape[1]))
    sum_query, sum_key, sum_value, sum_outgate, sum_decay_down = column_slices(
        sum_first, widths + (rank,)
    )
    sum_up, sum_attn, sum_mlp, sum_bias, sum_head = unpack_small(
        small_sums, small_shapes
    )
    return (
        block_output,
        input_grad,
        sum_attn,
        sum_query,
        sum_key,
        sum_value,
        sum_outgate,
        sum_decay_down,
        sum_up,
        sum_bias,
        sum_head,
        sum_out,
        sum_mlp,
        sum_gate,
        sum_up_proj,
        sum_down,
    )


def solution(mesh):
    return jax.shard_map(
        local,
        mesh=mesh,
        in_specs=(
            P("seq", None),
            P("seq", None),
            P("seq"),
            P("seq", None),
            P("seq", None),
            P("seq", None),
            P("seq", None),
            P("seq", None),
            P(None, "seq"),
            P("seq"),
            P("seq"),
            P("seq", None),
            P("seq"),
            P("seq", None),
            P("seq", None),
            P("seq", None),
        ),
        out_specs=(
            P("seq", None),
            P("seq", None),
            P("seq"),
            P("seq", None),
            P("seq", None),
            P("seq", None),
            P("seq", None),
            P("seq", None),
            P(None, "seq"),
            P("seq"),
            P("seq"),
            P("seq", None),
            P("seq"),
            P("seq", None),
            P("seq", None),
            P("seq", None),
        ),
        check_vma=False,
    )
```

```python
import jax
import jax.numpy as jnp
from jax import lax
from jax.experimental import pallas as pl
from jax.experimental.pallas import tpu as pltpu
from jax.sharding import PartitionSpec as P

H = 4
DK = 128
VALUE_WIDTH = 256
GROUP = 64


EPS = 1e-05
GATE_NORM = 16.0
TOP_PRECISION = lax.Precision.HIGHEST


LANES = 128


def pack_small(pieces):
    flat = jnp.concatenate([piece.reshape(-1) for piece in pieces])
    return jnp.pad(flat, (0, -flat.shape[0] % LANES))


def pack_small_sums(pieces, devices):
    flat = jnp.concatenate([piece.reshape(devices, -1) for piece in pieces], axis=1)
    return jnp.pad(flat, ((0, 0), (0, -flat.shape[1] % LANES)))


def unpack_small(flat, shapes):
    pieces, at = [], 0
    for shape in shapes:
        size = 1
        for extent in shape:
            size *= extent
        pieces.append(flat[..., at : at + size].reshape(flat.shape[:-1] + shape))
        at += size
    return pieces


def column_slices(array, widths):
    pieces, at = [], 0
    for width in widths:
        pieces.append(array[:, at : at + width])
        at += width
    return pieces


def neighbour_ring(count):
    if count % 8:
        return tuple(range(count))
    levels, order = count // 8, []
    for column, chip in enumerate((0, 1, 3, 2)):
        climb = range(levels) if column % 2 == 0 else range(levels - 1, -1, -1)
        for level in climb:
            order += [8 * level + 2 * chip, 8 * level + 2 * chip + 1]
    return tuple(order)


def in_vmem():
    return pl.BlockSpec(memory_space=pltpu.VMEM)


def prefix_body(states, logs, out):
    count = states.shape[0]
    carried = jnp.zeros(states.shape[1:], jnp.float32)
    for device in range(count):
        out[device] = carried.astype(out.dtype)
        fading = jnp.exp(logs[device].astype(jnp.float32).sum(axis=-1, keepdims=True))
        carried = fading * carried + states[device].astype(jnp.float32)


def suffix_body(states, logs, out):
    count = states.shape[0]
    carried = jnp.zeros(states.shape[1:], jnp.float32)
    for device in range(count - 1, -1, -1):
        out[device] = carried.astype(out.dtype)
        fading = jnp.exp(logs[device].astype(jnp.float32).sum(axis=-1, keepdims=True))
        carried = fading * carried + states[device].astype(jnp.float32)


def scan_devices(body, states, logs):
    return pl.pallas_call(
        body,
        out_shape=jax.ShapeDtypeStruct(states.shape, jnp.bfloat16),
        in_specs=[in_vmem(), in_vmem()],
        out_specs=in_vmem(),
    )(states, logs)


def exchange(array):
    return lax.all_to_all(array, "seq", 0, 0)


PLANE = 8
OFFSETS = (0, 2, 4, 6)


def plane_groups(count):
    return [list(range(start, start + PLANE)) for start in range(0, count, PLANE)]


def level_groups(count):
    return [list(range(place, count, PLANE)) for place in range(PLANE)]


def swapped(array, offset):
    count = lax.axis_size("seq")
    return lax.ppermute(array, "seq", [(device, device ^ offset) for device in range(count)])


def plane_gather(array):
    same = [array] + [swapped(array, offset) for offset in OFFSETS[1:]]
    return jnp.concatenate(same + [swapped(part, 1) for part in same], axis=0)


def plane_scatter(partial):
    return plane_scatter_rest(*plane_scatter_first(partial))


def plane_scatter_first(partial):
    half = partial.shape[0] // 2
    return partial[:half], partial[half:].astype(jnp.bfloat16)


def plane_scatter_rest(kept, sent):
    rows = kept.shape[0] // len(OFFSETS)
    joined = kept + swapped(sent, 1).astype(jnp.float32)
    total = joined[:rows]
    for place, offset in enumerate(OFFSETS[1:], 1):
        piece = joined[place * rows : (place + 1) * rows].astype(jnp.bfloat16)
        total = total + swapped(piece, offset).astype(jnp.float32)
    return total


def to_units(weight, levels, padded):
    rows, hidden = weight.shape
    width = hidden // (levels * PLANE)
    parts = weight.reshape(rows, levels, PLANE, width).transpose(2, 0, 1, 3)
    parts = parts.reshape(PLANE, rows, levels * width)
    return jnp.pad(parts, ((0, 0), (0, 0), (0, padded - levels * width)))


def from_units(parts, levels, hidden):
    rows = parts.shape[1]
    width = hidden // (levels * PLANE)
    parts = parts[:, :, : levels * width].reshape(PLANE, rows, levels, width)
    return parts.transpose(1, 2, 0, 3).reshape(rows, hidden)


def grads_body(normed, own_first, other_first, gated, own_hidden, other_hidden, out):
    tokens, start = own_first.shape[0], 0
    for left, own, other in ((normed, own_first, other_first), (gated, own_hidden, other_hidden)):
        for at in range(0, own.shape[1], 640):
            width = min(640, own.shape[1] - at)
            total = outer_sum(left[:tokens, :], own[:, at : at + width]) + outer_sum(
                left[tokens:, :], other[:, at : at + width]
            )
            out[:, start + at : start + at + width] = total.astype(out.dtype)
        start += own.shape[1]


def with_partner(array):
    return jnp.concatenate([array, swapped(array, 1)], axis=0)


def own_columns(array, chips, parity, rows):
    width = array.shape[1]
    column = jnp.arange(width // 2)
    place = jnp.asarray(chips, jnp.int32)[column // rows]
    source = (2 * place + parity) * rows + column % rows
    pick = jnp.arange(width)[:, None] == source[None, :]
    return jnp.dot(array, pick.astype(array.dtype), preferred_element_type=array.dtype)


def matmul(left_side, right_side):
    return jnp.dot(left_side, right_side, preferred_element_type=jnp.float32)


def times_back(left_side, right_side):
    return lax.dot_general(
        left_side, right_side, (((1,), (1,)), ((), ())), preferred_element_type=jnp.float32
    )


def outer_sum(left_side, right_side):
    return lax.dot_general(
        left_side, right_side, (((0,), (0,)), ((), ())), preferred_element_type=jnp.float32
    )


def rms_norm(matrix, gain):
    scaling = lax.rsqrt(jnp.mean(matrix * matrix, axis=-1, keepdims=True) + EPS)
    return matrix * scaling * gain


def swiglu(gate_pre, up_pre):
    return jax.nn.silu(gate_pre) * up_pre


def sized(left, right, contract, precision=TOP_PRECISION):
    return lax.dot_general(
        left, right, (contract, ((), ())), precision=precision, preferred_element_type=jnp.float32
    )


ROWS_BY_ROWS = ((0,), (0,))
COLUMNS_BY_COLUMNS = ((1,), (1,))
PLAIN = ((1,), (0,))


def triangle(size, lower=True):
    row = lax.broadcasted_iota(jnp.int32, (size, size), 0)
    column = lax.broadcasted_iota(jnp.int32, (size, size), 1)
    return (row >= column if lower else row <= column).astype(jnp.float32)


def log_decay_of(logit):
    return (jnp.minimum(logit, 0.0) - jnp.log1p(jnp.exp(-jnp.abs(logit)))) / GATE_NORM


def state_body(key, value, low, up, bias, logit_out, out):
    tokens, width = key.shape
    logit = sized(low[...].astype(jnp.bfloat16), up[...], PLAIN, None) + bias[...]
    logit_out[...] = logit
    log_decay = log_decay_of(logit)
    later = 1.0 - triangle(tokens)
    remaining = sized(later, log_decay, PLAIN)
    state = sized(key[...] * jnp.exp(remaining), value[...], ROWS_BY_ROWS)
    total = sized(log_decay, jnp.ones((tokens, LANES), jnp.float32), ROWS_BY_ROWS)
    high = total.astype(jnp.bfloat16).astype(jnp.float32)
    middle = (total - high).astype(jnp.bfloat16).astype(jnp.float32)
    lane = lax.broadcasted_iota(jnp.int32, (width, LANES), 1)
    pieces = jnp.where(lane == 0, high, jnp.where(lane == 1, middle, total - high - middle))
    out[:, : state.shape[1]] = state.astype(out.dtype)
    out[:, state.shape[1] :] = jnp.where(lane < 3, pieces, 0.0).astype(out.dtype)


def block_terms(query, key, log_decay):
    inner = sized(triangle(GROUP), log_decay, PLAIN)
    ending = inner[GROUP - 1 : GROUP, :]
    rising, falling = jnp.exp(inner), jnp.exp(-inner)
    fading = jnp.exp(ending - inner)
    return rising, falling, fading, query * rising, key * falling, key * fading


def ending_columns(log_decay, width):
    return jnp.exp(sized(log_decay, jnp.ones((log_decay.shape[0], width), jnp.float32), ROWS_BY_ROWS))


def output_body(query, key, value, logit, outgate, gain, entering, mixer_out, gated_out):
    state = entering[...].astype(jnp.float32)
    causal = triangle(GROUP)
    count = query.shape[0] // GROUP
    for block in range(count):
        at = slice(block * GROUP, (block + 1) * GROUP)
        log_decay = log_decay_of(logit[at, :])
        values = value[at, :]
        _, _, _, query_in, key_in, key_end = block_terms(
            query[at, :] * DK ** (-0.5), key[at, :], log_decay
        )
        scores = sized(query_in, key_in, COLUMNS_BY_COLUMNS) * causal
        mixer = sized(scores, values, PLAIN) + sized(query_in, state, PLAIN)
        if block < count - 1:
            state = ending_columns(log_decay, state.shape[1]) * state + sized(
                key_end, values, ROWS_BY_ROWS
            )
        mixer_out[at, :] = mixer
        scale = lax.rsqrt(jnp.mean(mixer * mixer, axis=-1, keepdims=True) + EPS)
        gate = outgate[at, :]
        gated_out[at, :] = (mixer * scale * gain[...] * gate * jax.nn.sigmoid(gate)).astype(
            gated_out.dtype
        )


def gate_back_body(
    d_gated, mixer, outgate, gain, query, logit, d_mixer_out, d_gate_out, gain_out, state_out
):
    tokens = query.shape[0]
    scale = lax.rsqrt(jnp.mean(mixer[...] * mixer[...], axis=-1, keepdims=True) + EPS)
    unit = mixer[...] * scale
    sigmoid = jax.nn.sigmoid(outgate[...])
    gradient = d_gated[...] * outgate[...] * sigmoid
    inward = gradient * gain[...]
    d_mixer = scale * (inward - unit * jnp.mean(inward * unit, axis=-1, keepdims=True))
    d_mixer_out[...] = d_mixer
    d_gate = d_gated[...] * unit * gain[...] * sigmoid * (1.0 + outgate[...] * (1.0 - sigmoid))
    d_gate_out[...] = d_gate.astype(d_gate_out.dtype)

    @pl.when(pl.program_id(0) == 0)
    def _():
        gain_out[...] = jnp.zeros(gain_out.shape, jnp.float32)

    gain_out[...] += jnp.sum(gradient * unit, axis=0, keepdims=True)
    cumulative = sized(triangle(tokens), log_decay_of(logit[...]), PLAIN)
    state_out[...] = sized(
        query[...] * (DK ** (-0.5)) * jnp.exp(cumulative), d_mixer, ROWS_BY_ROWS
    ).astype(state_out.dtype)


def mixer_back_body(
    query, key, value, logit, d_mixer, entering, leaving, d_gate, up, out, d_logit_out, bias_out, low
):
    head = pl.program_id(0)
    heads = pl.num_programs(0)
    width, value_width = key.shape[1], value.shape[1]
    count = query.shape[0] // GROUP
    causal, upper = triangle(GROUP), triangle(GROUP, lower=False)
    ones = jnp.ones((8, value_width), jnp.float32)
    state, blocks = entering[...].astype(jnp.float32), []
    for block in range(count):
        at = slice(block * GROUP, (block + 1) * GROUP)
        log_decay = log_decay_of(logit[at, :])
        terms = block_terms(query[at, :] * DK ** (-0.5), key[at, :], log_decay)
        factor = ending_columns(log_decay, value_width)
        blocks.append((at, terms, factor, state))
        if block < count - 1:
            state = factor * state + sized(terms[5], value[at, :], ROWS_BY_ROWS)
    d_state = leaving[...].astype(jnp.float32)
    bias_sum = jnp.zeros((1, width), jnp.float32)
    for at, terms, factor, state in reversed(blocks):
        rising, falling, fading, query_in, key_in, key_end = terms
        values, d_out = value[at, :], d_mixer[at, :]
        scores = sized(query_in, key_in, COLUMNS_BY_COLUMNS) * causal
        d_scores = sized(d_out, values, COLUMNS_BY_COLUMNS) * causal
        d_query_in = sized(d_scores, key_in, PLAIN) + sized(d_out, state, COLUMNS_BY_COLUMNS)
        d_key_in = sized(d_scores, query_in, ROWS_BY_ROWS)
        d_values = sized(scores, d_out, ROWS_BY_ROWS) + sized(key_end, d_state, PLAIN)
        d_key_end = sized(values, d_state, COLUMNS_BY_COLUMNS)
        d_ending = sized(ones, d_state * factor * state, COLUMNS_BY_COLUMNS)[0:1, :]
        end_part = d_key_end * key_end
        d_ending = d_ending + jnp.sum(end_part, axis=0, keepdims=True)
        d_inner = d_query_in * query_in - d_key_in * key_in - end_part
        d_log_decay = sized(upper, d_inner, PLAIN) + d_ending
        d_logit = d_log_decay * jax.nn.sigmoid(-logit[at, :]) / GATE_NORM
        bias_sum = bias_sum + jnp.sum(d_logit, axis=0, keepdims=True)
        d_logit_in = d_logit.astype(jnp.bfloat16)
        d_logit_out[at, :] = d_logit_in
        d_low = sized(d_logit_in, up[...], COLUMNS_BY_COLUMNS, None)
        d_low = jnp.where(head == 0, d_low, d_low + low[at, :])
        low[at, :] = d_low
        d_state = factor * d_state + sized(query_in, d_out, ROWS_BY_ROWS)
        at_query = pl.multiple_of(head * width, width)
        at_key = pl.multiple_of((heads + head) * width, width)
        at_value = pl.multiple_of(2 * heads * width + head * value_width, value_width)
        at_low = heads * (2 * width + value_width)
        at_gate = pl.multiple_of(at_low + LANES + head * value_width, LANES)
        out[at, pl.ds(at_query, width)] = (DK ** (-0.5) * d_query_in * rising).astype(out.dtype)
        out[at, pl.ds(at_key, width)] = (d_key_in * falling + d_key_end * fading).astype(out.dtype)
        out[at, pl.ds(at_value, value_width)] = d_values.astype(out.dtype)
        out[at, pl.ds(at_gate, value_width)] = d_gate[at, :]
        out[at, at_low : at_low + LANES] = d_low.astype(out.dtype)
    bias_out[...] = bias_sum


def per_head(rows, columns, offset=0):
    return pl.BlockSpec((rows, columns), lambda head: (0, head + offset))


def per_head_rows(rows, columns):
    return pl.BlockSpec((rows, columns), lambda head: (head, 0))


def whole_at(rows, columns, place):
    return pl.BlockSpec((rows, columns), lambda head: (0, place))


def whole(rows, columns):
    return pl.BlockSpec((rows, columns), lambda head: (0, 0))


def local(
    block_input,
    cotangent,
    attn_gain,
    w_query,
    w_key,
    w_value,
    w_outgate,
    w_decay_down,
    w_decay_up,
    decay_bias,
    head_gain,
    w_out,
    mlp_gain,
    w_gate,
    w_up,
    w_down,
):
    count = lax.axis_size("seq")
    rows = w_query.shape[0]
    key_width, value_width, rank = (w_query.shape[1], w_value.shape[1], w_decay_down.shape[1])
    hidden = w_gate.shape[1]
    small_shapes = (w_decay_up.shape, attn_gain.shape, mlp_gain.shape, decay_bias.shape, head_gain.shape)
    first = jnp.concatenate(
        [
            w_query,
            w_key,
            w_value,
            jnp.pad(w_decay_down, ((0, 0), (0, LANES - rank))),
        ],
        axis=1,
    )
    small = pack_small((w_decay_up, attn_gain, mlp_gain, decay_bias, head_gain))
    small = exchange(jnp.broadcast_to(small, (count, 1) + small.shape)).reshape(count, -1)
    first = lax.all_gather(first, "seq", axis=0, tiled=True)
    second = jnp.concatenate([w_outgate, w_out], axis=1)
    second = lax.all_gather(second, "seq", axis=0, tiled=True)
    levels = count // PLANE
    planes, columns = (plane_groups(count), level_groups(count))
    units = levels * w_down.shape[0]
    padded = -(-units // LANES) * LANES
    gate_up = jnp.concatenate([to_units(w_gate, levels, padded), to_units(w_up, levels, padded)], axis=2)
    gate_up = lax.all_to_all(gate_up, "seq", 0, 0, axis_index_groups=planes)
    gate_up = gate_up.reshape(PLANE * rows, 2 * padded)
    gate_up, first = lax.optimization_barrier((gate_up, first))
    gate_up = lax.all_gather(gate_up, "seq", axis=0, tiled=True, axis_index_groups=columns)
    down = lax.all_gather(w_down, "seq", axis=0, tiled=True, axis_index_groups=columns)
    down = jnp.pad(down, ((0, padded - units), (0, 0)))
    cot_in, first = lax.optimization_barrier((cotangent.astype(jnp.bfloat16), first))
    cot_plane = plane_gather(cot_in)
    wide = 2 * key_width + value_width
    up_pieces, attn_full, mlp_full_gain, bias_full, head_full = unpack_small(small, small_shapes)
    decay_up_full = up_pieces.transpose(1, 0, 2).reshape(rank, key_width)
    attn_full, mlp_full_gain, bias_full, head_full = (
        piece.reshape(-1).astype(jnp.float32) for piece in (attn_full, mlp_full_gain, bias_full, head_full)
    )
    scaling = DK ** (-0.5)
    normed, norm_back = jax.vjp(rms_norm, block_input, attn_full)
    normed_in = normed.astype(jnp.bfloat16)
    order = neighbour_ring(count)
    chips = tuple(device // 2 for device in order[::2])
    rings = [[2 * chip + core for chip in chips] for core in range(2)]
    parity = lax.axis_index("seq") % 2
    normed_pair = own_columns(with_partner(normed_in), chips, parity, rows)
    normed_in, down, normed_pair = lax.optimization_barrier((normed_in, down, normed_pair))
    wide_out = matmul(normed_in, first)
    tokens = wide_out.shape[0]
    up_rows = jnp.pad(decay_up_full, ((0, LANES - rank), (0, 0)))
    value_at = 2 * key_width // VALUE_WIDTH
    query_spec, key_spec = per_head(tokens, DK), per_head(tokens, DK, H)
    value_spec = per_head(tokens, VALUE_WIDTH, value_at)
    low_spec = whole_at(tokens, LANES, wide // LANES)
    up_spec = per_head(LANES, DK)
    head_values, head_keys = per_head(tokens, VALUE_WIDTH), per_head(tokens, DK)
    state_spec = per_head_rows(DK, VALUE_WIDTH)
    gain_spec = whole(1, VALUE_WIDTH)
    gain_row = head_full[None, :]
    chunk = key_width // count
    decay_logit, outgoing = pl.pallas_call(
        state_body,
        grid=(H,),
        in_specs=[key_spec, value_spec, low_spec, up_spec, per_head(1, DK)],
        out_specs=[head_keys, per_head_rows(DK, VALUE_WIDTH + LANES)],
        out_shape=[
            jax.ShapeDtypeStruct((tokens, key_width), jnp.float32),
            jax.ShapeDtypeStruct((key_width, VALUE_WIDTH + LANES), jnp.bfloat16),
        ],
    )(wide_out, wide_out, wide_out, up_rows, bias_full[None, :])
    arrived = exchange(outgoing.reshape(count, chunk, VALUE_WIDTH + LANES))
    logs = arrived[:, :, VALUE_WIDTH:]
    before = exchange(scan_devices(prefix_body, arrived[:, :, :VALUE_WIDTH], logs))
    before = before.reshape(key_width, VALUE_WIDTH)
    second, before = lax.optimization_barrier((second, before))
    outgate_full, out_full = column_slices(second, (value_width, w_out.shape[1]))
    outgate = matmul(normed_in, outgate_full)
    mixer, gated = pl.pallas_call(
        output_body,
        grid=(H,),
        in_specs=[query_spec, key_spec, value_spec, head_keys, head_values, gain_spec, state_spec],
        out_specs=[head_values, head_values],
        out_shape=[
            jax.ShapeDtypeStruct((tokens, value_width), jnp.float32),
            jax.ShapeDtypeStruct((tokens, value_width), jnp.bfloat16),
        ],
    )(wide_out, wide_out, wide_out, decay_logit, outgate, gain_row, before)
    gated_pair = own_columns(with_partner(gated), chips, parity, rows)
    hidden_state = block_input + matmul(gated, out_full)
    mlp_full, mlp_back = jax.vjp(rms_norm, hidden_state, mlp_full_gain)
    mlp_normed = mlp_full.astype(jnp.bfloat16)
    mlp_plane = plane_gather(mlp_normed)
    gate_pre, up_pre = column_slices(matmul(mlp_plane, gate_up), (padded, padded))
    activ_full, activ_back = jax.vjp(swiglu, gate_pre, up_pre)
    activ = activ_full.astype(jnp.bfloat16)
    d_activ = times_back(cot_plane, down)
    d_gate_full, d_up_full = activ_back(d_activ)
    d_gate_up = jnp.concatenate(
        [d_gate_full.astype(jnp.bfloat16), d_up_full.astype(jnp.bfloat16)], axis=1
    )
    d_mlp_normed = plane_scatter(times_back(d_gate_up, gate_up))

    def level_sum(partial):
        return lax.psum_scatter(
            partial.astype(jnp.bfloat16),
            "seq",
            scatter_dimension=0,
            tiled=True,
            axis_index_groups=columns,
        )

    sum_down = level_sum(outer_sum(activ, cot_plane)[:units]).astype(jnp.float32)
    sum_gate_up = level_sum(outer_sum(mlp_plane, d_gate_up)).reshape(PLANE, rows, 2 * padded)
    sum_gate_up = lax.all_to_all(sum_gate_up, "seq", 0, 0, axis_index_groups=planes)
    sum_gate_up = sum_gate_up.astype(jnp.float32)
    sum_gate = from_units(sum_gate_up[:, :, :padded], levels, hidden)
    sum_up_proj = from_units(sum_gate_up[:, :, padded:], levels, hidden)
    d_hidden_norm, grad_mlp_gain = mlp_back(d_mlp_normed)
    d_hidden = cotangent + d_hidden_norm
    d_hidden_in, gated_pair = lax.optimization_barrier((d_hidden.astype(jnp.bfloat16), gated_pair))
    hidden_other = swapped(d_hidden_in, 1)
    d_gated = times_back(d_hidden_in, out_full)
    mixer_gradient, d_outgate, grad_head_gain, state_gradient = pl.pallas_call(
        gate_back_body,
        grid=(H,),
        in_specs=[head_values, head_values, head_values, gain_spec, query_spec, head_keys],
        out_specs=[head_values, head_values, gain_spec, state_spec],
        out_shape=[
            jax.ShapeDtypeStruct((tokens, value_width), jnp.float32),
            jax.ShapeDtypeStruct((tokens, value_width), jnp.bfloat16),
            jax.ShapeDtypeStruct((1, VALUE_WIDTH), jnp.float32),
            jax.ShapeDtypeStruct((key_width, VALUE_WIDTH), jnp.bfloat16),
        ],
    )(d_gated, mixer, outgate, gain_row, wide_out, decay_logit)
    activ_late, state_gradient = lax.optimization_barrier((activ, state_gradient))
    arrived_back = exchange(state_gradient.reshape(count, chunk, VALUE_WIDTH))
    after = exchange(scan_devices(suffix_body, arrived_back, logs))
    kept, sent = plane_scatter_first(matmul(activ_late, down))
    kept, sent, after = lax.optimization_barrier((kept, sent, after))
    block_output = hidden_state + plane_scatter_rest(kept, sent)
    after = after.reshape(key_width, VALUE_WIDTH)
    d_first, d_logit_in, grad_decay_bias = pl.pallas_call(
        mixer_back_body,
        grid=(H,),
        in_specs=[
            query_spec,
            key_spec,
            value_spec,
            head_keys,
            head_values,
            state_spec,
            state_spec,
            head_values,
            up_spec,
        ],
        out_specs=[whole(tokens, wide + LANES + value_width), head_keys, per_head(1, DK)],
        out_shape=[
            jax.ShapeDtypeStruct((tokens, wide + LANES + value_width), jnp.bfloat16),
            jax.ShapeDtypeStruct((tokens, key_width), jnp.bfloat16),
            jax.ShapeDtypeStruct((1, key_width), jnp.float32),
        ],
        scratch_shapes=[pltpu.VMEM((tokens, LANES), jnp.float32)],
    )(
        wide_out,
        wide_out,
        wide_out,
        decay_logit,
        mixer_gradient,
        before,
        after,
        d_outgate,
        up_rows,
    )
    low_rank = wide_out[:, wide : wide + rank].astype(jnp.bfloat16)
    grad_decay_up = outer_sum(low_rank, d_logit_in)
    d_normed = times_back(d_first[:, : wide + LANES], first)
    d_normed = d_normed + times_back(d_first[:, wide + LANES :], outgate_full)
    d_input_norm, grad_attn_gain = norm_back(d_normed)
    input_grad = d_hidden + d_input_norm

    small_sums = pack_small_sums(
        (
            grad_decay_up.reshape(rank, count, -1).transpose(1, 0, 2),
            grad_attn_gain,
            grad_mlp_gain,
            grad_decay_bias,
            grad_head_gain.reshape(-1),
        ),
        count,
    )
    small_sums = jnp.sum(exchange(small_sums), axis=0)
    sums = pl.pallas_call(
        grads_body,
        in_specs=[in_vmem()] * 6,
        out_specs=in_vmem(),
        out_shape=jax.ShapeDtypeStruct(
            (normed_pair.shape[1], d_first.shape[1] + d_hidden_in.shape[1]), jnp.bfloat16
        ),
    )(normed_pair, d_first, swapped(d_first, 1), gated_pair, d_hidden_in, hidden_other)
    sums = lax.psum_scatter(
        sums, "seq", scatter_dimension=0, tiled=True, axis_index_groups=rings
    ).astype(jnp.float32)
    sum_query, sum_key, sum_value, sum_decay_down, sum_outgate, sum_out = column_slices(
        sums, (key_width, key_width, value_width, LANES, value_width, w_out.shape[1])
    )
    sum_decay_down = sum_decay_down[:, :rank]
    sum_up, sum_attn, sum_mlp, sum_bias, sum_head = unpack_small(
        small_sums, small_shapes
    )
    return (
        block_output,
        input_grad,
        sum_attn,
        sum_query,
        sum_key,
        sum_value,
        sum_outgate,
        sum_decay_down,
        sum_up,
        sum_bias,
        sum_head,
        sum_out,
        sum_mlp,
        sum_gate,
        sum_up_proj,
        sum_down,
    )


def solution(mesh):
    return jax.shard_map(
        local,
        mesh=mesh,
        in_specs=(
            P("seq", None),
            P("seq", None),
            P("seq"),
            P("seq", None),
            P("seq", None),
            P("seq", None),
            P("seq", None),
            P("seq", None),
            P(None, "seq"),
            P("seq"),
            P("seq"),
            P("seq", None),
            P("seq"),
            P("seq", None),
            P("seq", None),
            P("seq", None),
        ),
        out_specs=(
            P("seq", None),
            P("seq", None),
            P("seq"),
            P("seq", None),
            P("seq", None),
            P("seq", None),
            P("seq", None),
            P("seq", None),
            P(None, "seq"),
            P("seq"),
            P("seq"),
            P("seq", None),
            P("seq"),
            P("seq", None),
            P("seq", None),
            P("seq", None),
        ),
        check_vma=False,
    )
```

```python
import jax
import jax.numpy as jnp
from jax import lax
from jax.experimental import pallas as pl
from jax.experimental.pallas import tpu as pltpu
from jax.sharding import PartitionSpec as P

H = 4
DK = 128
VALUE_WIDTH = 256
GROUP = 64


EPS = 1e-05
GATE_NORM = 16.0
TOP_PRECISION = lax.Precision.HIGHEST


LANES = 128


def pack_small(pieces):
    flat = jnp.concatenate([piece.reshape(-1) for piece in pieces])
    return jnp.pad(flat, (0, -flat.shape[0] % LANES))


def pack_small_sums(pieces, devices):
    flat = jnp.concatenate([piece.reshape(devices, -1) for piece in pieces], axis=1)
    return jnp.pad(flat, ((0, 0), (0, -flat.shape[1] % LANES)))


def unpack_small(flat, shapes):
    pieces, at = [], 0
    for shape in shapes:
        size = 1
        for extent in shape:
            size *= extent
        pieces.append(flat[..., at : at + size].reshape(flat.shape[:-1] + shape))
        at += size
    return pieces


def column_slices(array, widths):
    pieces, at = [], 0
    for width in widths:
        pieces.append(array[:, at : at + width])
        at += width
    return pieces


def neighbour_ring(count):
    if count % 8:
        return tuple(range(count))
    levels, order = count // 8, []
    for column, chip in enumerate((0, 1, 3, 2)):
        climb = range(levels) if column % 2 == 0 else range(levels - 1, -1, -1)
        for level in climb:
            order += [8 * level + 2 * chip, 8 * level + 2 * chip + 1]
    return tuple(order)


def in_vmem():
    return pl.BlockSpec(memory_space=pltpu.VMEM)


def prefix_body(states, logs, out):
    count = states.shape[0]
    carried = jnp.zeros(states.shape[1:], jnp.float32)
    for device in range(count):
        out[device] = carried.astype(out.dtype)
        fading = jnp.exp(logs[device].astype(jnp.float32).sum(axis=-1, keepdims=True))
        carried = fading * carried + states[device].astype(jnp.float32)


def suffix_body(states, logs, out):
    count = states.shape[0]
    carried = jnp.zeros(states.shape[1:], jnp.float32)
    for device in range(count - 1, -1, -1):
        out[device] = carried.astype(out.dtype)
        fading = jnp.exp(logs[device].astype(jnp.float32).sum(axis=-1, keepdims=True))
        carried = fading * carried + states[device].astype(jnp.float32)


def scan_devices(body, states, logs):
    return pl.pallas_call(
        body,
        out_shape=jax.ShapeDtypeStruct(states.shape, jnp.bfloat16),
        in_specs=[in_vmem(), in_vmem()],
        out_specs=in_vmem(),
    )(states, logs)


def exchange(array):
    return lax.all_to_all(array, "seq", 0, 0)


PLANE = 8
OFFSETS = (0, 2, 4, 6)


def plane_groups(count):
    return [list(range(start, start + PLANE)) for start in range(0, count, PLANE)]


def level_groups(count):
    return [list(range(place, count, PLANE)) for place in range(PLANE)]


def swapped(array, offset):
    count = lax.axis_size("seq")
    return lax.ppermute(array, "seq", [(device, device ^ offset) for device in range(count)])


def plane_gather(array):
    same = [array] + [swapped(array, offset) for offset in OFFSETS[1:]]
    return jnp.concatenate(same + [swapped(part, 1) for part in same], axis=0)


def plane_scatter(partial):
    return plane_scatter_rest(*plane_scatter_first(partial))


def plane_scatter_first(partial):
    half = partial.shape[0] // 2
    return partial[:half], partial[half:].astype(jnp.bfloat16)


def plane_scatter_rest(kept, sent):
    rows = kept.shape[0] // len(OFFSETS)
    joined = kept + swapped(sent, 1).astype(jnp.float32)
    total = joined[:rows]
    for place, offset in enumerate(OFFSETS[1:], 1):
        piece = joined[place * rows : (place + 1) * rows].astype(jnp.bfloat16)
        total = total + swapped(piece, offset).astype(jnp.float32)
    return total


def to_units(weight, levels, padded):
    rows, hidden = weight.shape
    width = hidden // (levels * PLANE)
    parts = weight.reshape(rows, levels, PLANE, width).transpose(2, 0, 1, 3)
    parts = parts.reshape(PLANE, rows, levels * width)
    return jnp.pad(parts, ((0, 0), (0, 0), (0, padded - levels * width)))


def from_units(parts, levels, hidden):
    rows = parts.shape[1]
    width = hidden // (levels * PLANE)
    parts = parts[:, :, : levels * width].reshape(PLANE, rows, levels, width)
    return parts.transpose(1, 2, 0, 3).reshape(rows, hidden)


def grads_body(normed, own_first, other_first, gated, own_hidden, other_hidden, out):
    tokens, start = own_first.shape[0], 0
    for left, own, other in ((normed, own_first, other_first), (gated, own_hidden, other_hidden)):
        for at in range(0, own.shape[1], 640):
            width = min(640, own.shape[1] - at)
            total = outer_sum(left[:tokens, :], own[:, at : at + width]) + outer_sum(
                left[tokens:, :], other[:, at : at + width]
            )
            out[:, start + at : start + at + width] = total.astype(out.dtype)
        start += own.shape[1]


def with_partner(array):
    return jnp.concatenate([array, swapped(array, 1)], axis=0)


def own_columns(array, chips, parity, rows):
    width = array.shape[1]
    column = jnp.arange(width // 2)
    place = jnp.asarray(chips, jnp.int32)[column // rows]
    source = (2 * place + parity) * rows + column % rows
    pick = jnp.arange(width)[:, None] == source[None, :]
    return jnp.dot(array, pick.astype(array.dtype), preferred_element_type=array.dtype)


def matmul(left_side, right_side):
    return jnp.dot(left_side, right_side, preferred_element_type=jnp.float32)


def times_back(left_side, right_side):
    return lax.dot_general(
        left_side, right_side, (((1,), (1,)), ((), ())), preferred_element_type=jnp.float32
    )


def outer_sum(left_side, right_side):
    return lax.dot_general(
        left_side, right_side, (((0,), (0,)), ((), ())), preferred_element_type=jnp.float32
    )


def rms_norm(matrix, gain):
    scaling = lax.rsqrt(jnp.mean(matrix * matrix, axis=-1, keepdims=True) + EPS)
    return matrix * scaling * gain


def swiglu(gate_pre, up_pre):
    return jax.nn.silu(gate_pre) * up_pre


def sized(left, right, contract, precision=TOP_PRECISION):
    return lax.dot_general(
        left, right, (contract, ((), ())), precision=precision, preferred_element_type=jnp.float32
    )


ROWS_BY_ROWS = ((0,), (0,))
COLUMNS_BY_COLUMNS = ((1,), (1,))
PLAIN = ((1,), (0,))


def triangle(size, lower=True):
    row = lax.broadcasted_iota(jnp.int32, (size, size), 0)
    column = lax.broadcasted_iota(jnp.int32, (size, size), 1)
    return (row >= column if lower else row <= column).astype(jnp.float32)


def log_decay_of(logit):
    return (jnp.minimum(logit, 0.0) - jnp.log1p(jnp.exp(-jnp.abs(logit)))) / GATE_NORM


def state_body(key, value, low, up, bias, logit_out, out):
    tokens, width = key.shape
    logit = sized(low[...].astype(jnp.bfloat16), up[...], PLAIN, None) + bias[...]
    logit_out[...] = logit
    log_decay = log_decay_of(logit)
    later = 1.0 - triangle(tokens)
    remaining = sized(later, log_decay, PLAIN)
    state = sized(key[...] * jnp.exp(remaining), value[...], ROWS_BY_ROWS)
    total = sized(log_decay, jnp.ones((tokens, LANES), jnp.float32), ROWS_BY_ROWS)
    high = total.astype(jnp.bfloat16).astype(jnp.float32)
    middle = (total - high).astype(jnp.bfloat16).astype(jnp.float32)
    lane = lax.broadcasted_iota(jnp.int32, (width, LANES), 1)
    pieces = jnp.where(lane == 0, high, jnp.where(lane == 1, middle, total - high - middle))
    out[:, : state.shape[1]] = state.astype(out.dtype)
    out[:, state.shape[1] :] = jnp.where(lane < 3, pieces, 0.0).astype(out.dtype)


def block_terms(query, key, log_decay):
    inner = sized(triangle(GROUP), log_decay, PLAIN)
    ending = inner[GROUP - 1 : GROUP, :]
    rising, falling = jnp.exp(inner), jnp.exp(-inner)
    fading = jnp.exp(ending - inner)
    return rising, falling, fading, query * rising, key * falling, key * fading


def ending_columns(log_decay, width):
    return jnp.exp(sized(log_decay, jnp.ones((log_decay.shape[0], width), jnp.float32), ROWS_BY_ROWS))


def output_body(query, key, value, logit, outgate, gain, entering, mixer_out, gated_out):
    state = entering[...].astype(jnp.float32)
    causal = triangle(GROUP)
    count = query.shape[0] // GROUP
    for block in range(count):
        at = slice(block * GROUP, (block + 1) * GROUP)
        log_decay = log_decay_of(logit[at, :])
        values = value[at, :]
        _, _, _, query_in, key_in, key_end = block_terms(
            query[at, :] * DK ** (-0.5), key[at, :], log_decay
        )
        scores = sized(query_in, key_in, COLUMNS_BY_COLUMNS) * causal
        mixer = sized(scores, values, PLAIN) + sized(query_in, state, PLAIN)
        if block < count - 1:
            state = ending_columns(log_decay, state.shape[1]) * state + sized(
                key_end, values, ROWS_BY_ROWS
            )
        mixer_out[at, :] = mixer
        scale = lax.rsqrt(jnp.mean(mixer * mixer, axis=-1, keepdims=True) + EPS)
        gate = outgate[at, :]
        gated_out[at, :] = (mixer * scale * gain[...] * gate * jax.nn.sigmoid(gate)).astype(
            gated_out.dtype
        )


def gate_back_body(
    d_gated, mixer, outgate, gain, query, logit, d_mixer_out, d_gate_out, gain_out, state_out
):
    tokens = query.shape[0]
    scale = lax.rsqrt(jnp.mean(mixer[...] * mixer[...], axis=-1, keepdims=True) + EPS)
    unit = mixer[...] * scale
    sigmoid = jax.nn.sigmoid(outgate[...])
    gradient = d_gated[...] * outgate[...] * sigmoid
    inward = gradient * gain[...]
    d_mixer = scale * (inward - unit * jnp.mean(inward * unit, axis=-1, keepdims=True))
    d_mixer_out[...] = d_mixer
    d_gate = d_gated[...] * unit * gain[...] * sigmoid * (1.0 + outgate[...] * (1.0 - sigmoid))
    d_gate_out[...] = d_gate.astype(d_gate_out.dtype)

    @pl.when(pl.program_id(0) == 0)
    def _():
        gain_out[...] = jnp.zeros(gain_out.shape, jnp.float32)

    gain_out[...] += jnp.sum(gradient * unit, axis=0, keepdims=True)
    cumulative = sized(triangle(tokens), log_decay_of(logit[...]), PLAIN)
    state_out[...] = sized(
        query[...] * (DK ** (-0.5)) * jnp.exp(cumulative), d_mixer, ROWS_BY_ROWS
    ).astype(state_out.dtype)


def mixer_back_body(
    query, key, value, logit, d_mixer, entering, leaving, d_gate, up, out, d_logit_out, bias_out, low
):
    head = pl.program_id(0)
    heads = pl.num_programs(0)
    width, value_width = key.shape[1], value.shape[1]
    count = query.shape[0] // GROUP
    causal, upper = triangle(GROUP), triangle(GROUP, lower=False)
    ones = jnp.ones((8, value_width), jnp.float32)
    state, blocks = entering[...].astype(jnp.float32), []
    for block in range(count):
        at = slice(block * GROUP, (block + 1) * GROUP)
        log_decay = log_decay_of(logit[at, :])
        terms = block_terms(query[at, :] * DK ** (-0.5), key[at, :], log_decay)
        factor = ending_columns(log_decay, value_width)
        blocks.append((at, terms, factor, state))
        if block < count - 1:
            state = factor * state + sized(terms[5], value[at, :], ROWS_BY_ROWS)
    d_state = leaving[...].astype(jnp.float32)
    bias_sum = jnp.zeros((1, width), jnp.float32)
    for at, terms, factor, state in reversed(blocks):
        rising, falling, fading, query_in, key_in, key_end = terms
        values, d_out = value[at, :], d_mixer[at, :]
        scores = sized(query_in, key_in, COLUMNS_BY_COLUMNS) * causal
        d_scores = sized(d_out, values, COLUMNS_BY_COLUMNS) * causal
        d_query_in = sized(d_scores, key_in, PLAIN) + sized(d_out, state, COLUMNS_BY_COLUMNS)
        d_key_in = sized(d_scores, query_in, ROWS_BY_ROWS)
        d_values = sized(scores, d_out, ROWS_BY_ROWS) + sized(key_end, d_state, PLAIN)
        d_key_end = sized(values, d_state, COLUMNS_BY_COLUMNS)
        d_ending = sized(ones, d_state * factor * state, COLUMNS_BY_COLUMNS)[0:1, :]
        end_part = d_key_end * key_end
        d_ending = d_ending + jnp.sum(end_part, axis=0, keepdims=True)
        d_inner = d_query_in * query_in - d_key_in * key_in - end_part
        d_log_decay = sized(upper, d_inner, PLAIN) + d_ending
        d_logit = d_log_decay * jax.nn.sigmoid(-logit[at, :]) / GATE_NORM
        bias_sum = bias_sum + jnp.sum(d_logit, axis=0, keepdims=True)
        d_logit_in = d_logit.astype(jnp.bfloat16)
        d_logit_out[at, :] = d_logit_in
        d_low = sized(d_logit_in, up[...], COLUMNS_BY_COLUMNS, None)
        d_low = jnp.where(head == 0, d_low, d_low + low[at, :])
        low[at, :] = d_low
        d_state = factor * d_state + sized(query_in, d_out, ROWS_BY_ROWS)
        at_query = pl.multiple_of(head * width, width)
        at_key = pl.multiple_of((heads + head) * width, width)
        at_value = pl.multiple_of(2 * heads * width + head * value_width, value_width)
        at_low = heads * (2 * width + value_width)
        at_gate = pl.multiple_of(at_low + LANES + head * value_width, LANES)
        out[at, pl.ds(at_query, width)] = (DK ** (-0.5) * d_query_in * rising).astype(out.dtype)
        out[at, pl.ds(at_key, width)] = (d_key_in * falling + d_key_end * fading).astype(out.dtype)
        out[at, pl.ds(at_value, value_width)] = d_values.astype(out.dtype)
        out[at, pl.ds(at_gate, value_width)] = d_gate[at, :]
        out[at, at_low : at_low + LANES] = d_low.astype(out.dtype)
    bias_out[...] = bias_sum


def per_head(rows, columns, offset=0):
    return pl.BlockSpec((rows, columns), lambda head: (0, head + offset))


def per_head_rows(rows, columns):
    return pl.BlockSpec((rows, columns), lambda head: (head, 0))


def whole_at(rows, columns, place):
    return pl.BlockSpec((rows, columns), lambda head: (0, place))


def whole(rows, columns):
    return pl.BlockSpec((rows, columns), lambda head: (0, 0))


def local(
    block_input,
    cotangent,
    attn_gain,
    w_query,
    w_key,
    w_value,
    w_outgate,
    w_decay_down,
    w_decay_up,
    decay_bias,
    head_gain,
    w_out,
    mlp_gain,
    w_gate,
    w_up,
    w_down,
):
    count = lax.axis_size("seq")
    rows = w_query.shape[0]
    key_width, value_width, rank = (w_query.shape[1], w_value.shape[1], w_decay_down.shape[1])
    hidden = w_gate.shape[1]
    small_shapes = (w_decay_up.shape, attn_gain.shape, mlp_gain.shape, decay_bias.shape, head_gain.shape)
    first = jnp.concatenate(
        [
            w_query,
            w_key,
            w_value,
            jnp.pad(w_decay_down, ((0, 0), (0, LANES - rank))),
            w_outgate,
        ],
        axis=1,
    )
    small = pack_small((w_decay_up, attn_gain, mlp_gain, decay_bias, head_gain))
    small = exchange(jnp.broadcast_to(small, (count, 1) + small.shape)).reshape(count, -1)
    first = lax.all_gather(first, "seq", axis=0, tiled=True)
    out_full = lax.all_gather(w_out, "seq", axis=0, tiled=True)
    levels = count // PLANE
    planes, columns = (plane_groups(count), level_groups(count))
    units = levels * w_down.shape[0]
    padded = -(-units // LANES) * LANES
    gate_up = jnp.concatenate([to_units(w_gate, levels, padded), to_units(w_up, levels, padded)], axis=2)
    gate_up = lax.all_to_all(gate_up, "seq", 0, 0, axis_index_groups=planes)
    gate_up = gate_up.reshape(PLANE * rows, 2 * padded)
    gate_up, first = lax.optimization_barrier((gate_up, first))
    gate_up = lax.all_gather(gate_up, "seq", axis=0, tiled=True, axis_index_groups=columns)
    down = lax.all_gather(w_down, "seq", axis=0, tiled=True, axis_index_groups=columns)
    down = jnp.pad(down, ((0, padded - units), (0, 0)))
    cot_in, first = lax.optimization_barrier((cotangent.astype(jnp.bfloat16), first))
    cot_plane = plane_gather(cot_in)
    wide = 2 * key_width + value_width
    up_pieces, attn_full, mlp_full_gain, bias_full, head_full = unpack_small(small, small_shapes)
    decay_up_full = up_pieces.transpose(1, 0, 2).reshape(rank, key_width)
    attn_full, mlp_full_gain, bias_full, head_full = (
        piece.reshape(-1).astype(jnp.float32) for piece in (attn_full, mlp_full_gain, bias_full, head_full)
    )
    scaling = DK ** (-0.5)
    normed, norm_back = jax.vjp(rms_norm, block_input, attn_full)
    normed_in = normed.astype(jnp.bfloat16)
    order = neighbour_ring(count)
    chips = tuple(device // 2 for device in order[::2])
    rings = [[2 * chip + core for chip in chips] for core in range(2)]
    parity = lax.axis_index("seq") % 2
    normed_pair = own_columns(with_partner(normed_in), chips, parity, rows)
    normed_in, down, normed_pair = lax.optimization_barrier((normed_in, down, normed_pair))
    wide_out = matmul(normed_in, first[:, : wide + LANES])
    tokens = wide_out.shape[0]
    up_rows = jnp.pad(decay_up_full, ((0, LANES - rank), (0, 0)))
    value_at = 2 * key_width // VALUE_WIDTH
    query_spec, key_spec = per_head(tokens, DK), per_head(tokens, DK, H)
    value_spec = per_head(tokens, VALUE_WIDTH, value_at)
    low_spec = whole_at(tokens, LANES, wide // LANES)
    up_spec = per_head(LANES, DK)
    head_values, head_keys = per_head(tokens, VALUE_WIDTH), per_head(tokens, DK)
    state_spec = per_head_rows(DK, VALUE_WIDTH)
    gain_spec = whole(1, VALUE_WIDTH)
    gain_row = head_full[None, :]
    chunk = key_width // count
    decay_logit, outgoing = pl.pallas_call(
        state_body,
        grid=(H,),
        in_specs=[key_spec, value_spec, low_spec, up_spec, per_head(1, DK)],
        out_specs=[head_keys, per_head_rows(DK, VALUE_WIDTH + LANES)],
        out_shape=[
            jax.ShapeDtypeStruct((tokens, key_width), jnp.float32),
            jax.ShapeDtypeStruct((key_width, VALUE_WIDTH + LANES), jnp.bfloat16),
        ],
    )(wide_out, wide_out, wide_out, up_rows, bias_full[None, :])
    arrived = exchange(outgoing.reshape(count, chunk, VALUE_WIDTH + LANES))
    logs = arrived[:, :, VALUE_WIDTH:]
    before = exchange(scan_devices(prefix_body, arrived[:, :, :VALUE_WIDTH], logs))
    before = before.reshape(key_width, VALUE_WIDTH)
    outgate = matmul(normed_in, first[:, wide + LANES :])
    mixer, gated = pl.pallas_call(
        output_body,
        grid=(H,),
        in_specs=[query_spec, key_spec, value_spec, head_keys, head_values, gain_spec, state_spec],
        out_specs=[head_values, head_values],
        out_shape=[
            jax.ShapeDtypeStruct((tokens, value_width), jnp.float32),
            jax.ShapeDtypeStruct((tokens, value_width), jnp.bfloat16),
        ],
    )(wide_out, wide_out, wide_out, decay_logit, outgate, gain_row, before)
    gated_pair = own_columns(with_partner(gated), chips, parity, rows)
    hidden_state = block_input + matmul(gated, out_full)
    mlp_full, mlp_back = jax.vjp(rms_norm, hidden_state, mlp_full_gain)
    mlp_normed = mlp_full.astype(jnp.bfloat16)
    mlp_plane = plane_gather(mlp_normed)
    gate_pre, up_pre = column_slices(matmul(mlp_plane, gate_up), (padded, padded))
    activ_full, activ_back = jax.vjp(swiglu, gate_pre, up_pre)
    activ = activ_full.astype(jnp.bfloat16)
    d_activ = times_back(cot_plane, down)
    d_gate_full, d_up_full = activ_back(d_activ)
    d_gate_up = jnp.concatenate(
        [d_gate_full.astype(jnp.bfloat16), d_up_full.astype(jnp.bfloat16)], axis=1
    )
    d_mlp_normed = plane_scatter(times_back(d_gate_up, gate_up))

    def level_sum(partial):
        return lax.psum_scatter(
            partial.astype(jnp.bfloat16),
            "seq",
            scatter_dimension=0,
            tiled=True,
            axis_index_groups=columns,
        )

    sum_down = level_sum(outer_sum(activ, cot_plane)[:units]).astype(jnp.float32)
    sum_gate_up = level_sum(outer_sum(mlp_plane, d_gate_up)).reshape(PLANE, rows, 2 * padded)
    sum_gate_up = lax.all_to_all(sum_gate_up, "seq", 0, 0, axis_index_groups=planes)
    sum_gate_up = sum_gate_up.astype(jnp.float32)
    sum_gate = from_units(sum_gate_up[:, :, :padded], levels, hidden)
    sum_up_proj = from_units(sum_gate_up[:, :, padded:], levels, hidden)
    d_hidden_norm, grad_mlp_gain = mlp_back(d_mlp_normed)
    d_hidden = cotangent + d_hidden_norm
    d_hidden_in, gated_pair = lax.optimization_barrier((d_hidden.astype(jnp.bfloat16), gated_pair))
    hidden_other = swapped(d_hidden_in, 1)
    d_gated = times_back(d_hidden_in, out_full)
    mixer_gradient, d_outgate, grad_head_gain, state_gradient = pl.pallas_call(
        gate_back_body,
        grid=(H,),
        in_specs=[head_values, head_values, head_values, gain_spec, query_spec, head_keys],
        out_specs=[head_values, head_values, gain_spec, state_spec],
        out_shape=[
            jax.ShapeDtypeStruct((tokens, value_width), jnp.float32),
            jax.ShapeDtypeStruct((tokens, value_width), jnp.bfloat16),
            jax.ShapeDtypeStruct((1, VALUE_WIDTH), jnp.float32),
            jax.ShapeDtypeStruct((key_width, VALUE_WIDTH), jnp.bfloat16),
        ],
    )(d_gated, mixer, outgate, gain_row, wide_out, decay_logit)
    activ_late, state_gradient = lax.optimization_barrier((activ, state_gradient))
    arrived_back = exchange(state_gradient.reshape(count, chunk, VALUE_WIDTH))
    after = exchange(scan_devices(suffix_body, arrived_back, logs))
    kept, sent = plane_scatter_first(matmul(activ_late, down))
    kept, sent, after = lax.optimization_barrier((kept, sent, after))
    block_output = hidden_state + plane_scatter_rest(kept, sent)
    after = after.reshape(key_width, VALUE_WIDTH)
    d_first, d_logit_in, grad_decay_bias = pl.pallas_call(
        mixer_back_body,
        grid=(H,),
        in_specs=[
            query_spec,
            key_spec,
            value_spec,
            head_keys,
            head_values,
            state_spec,
            state_spec,
            head_values,
            up_spec,
        ],
        out_specs=[whole(tokens, wide + LANES + value_width), head_keys, per_head(1, DK)],
        out_shape=[
            jax.ShapeDtypeStruct((tokens, wide + LANES + value_width), jnp.bfloat16),
            jax.ShapeDtypeStruct((tokens, key_width), jnp.bfloat16),
            jax.ShapeDtypeStruct((1, key_width), jnp.float32),
        ],
        scratch_shapes=[pltpu.VMEM((tokens, LANES), jnp.float32)],
    )(
        wide_out,
        wide_out,
        wide_out,
        decay_logit,
        mixer_gradient,
        before,
        after,
        d_outgate,
        up_rows,
    )
    low_rank = wide_out[:, wide : wide + rank].astype(jnp.bfloat16)
    grad_decay_up = outer_sum(low_rank, d_logit_in)
    d_normed = times_back(d_first, first)
    d_input_norm, grad_attn_gain = norm_back(d_normed)
    input_grad = d_hidden + d_input_norm

    small_sums = pack_small_sums(
        (
            grad_decay_up.reshape(rank, count, -1).transpose(1, 0, 2),
            grad_attn_gain,
            grad_mlp_gain,
            grad_decay_bias,
            grad_head_gain.reshape(-1),
        ),
        count,
    )
    small_sums = jnp.sum(exchange(small_sums), axis=0)
    sums = pl.pallas_call(
        grads_body,
        in_specs=[in_vmem()] * 6,
        out_specs=in_vmem(),
        out_shape=jax.ShapeDtypeStruct(
            (normed_pair.shape[1], d_first.shape[1] + d_hidden_in.shape[1]), jnp.bfloat16
        ),
    )(normed_pair, d_first, swapped(d_first, 1), gated_pair, d_hidden_in, hidden_other)
    sums = lax.psum_scatter(
        sums, "seq", scatter_dimension=0, tiled=True, axis_index_groups=rings
    ).astype(jnp.float32)
    sum_query, sum_key, sum_value, sum_decay_down, sum_outgate, sum_out = column_slices(
        sums, (key_width, key_width, value_width, LANES, value_width, w_out.shape[1])
    )
    sum_decay_down = sum_decay_down[:, :rank]
    sum_up, sum_attn, sum_mlp, sum_bias, sum_head = unpack_small(
        small_sums, small_shapes
    )
    return (
        block_output,
        input_grad,
        sum_attn,
        sum_query,
        sum_key,
        sum_value,
        sum_outgate,
        sum_decay_down,
        sum_up,
        sum_bias,
        sum_head,
        sum_out,
        sum_mlp,
        sum_gate,
        sum_up_proj,
        sum_down,
    )


def solution(mesh):
    return jax.shard_map(
        local,
        mesh=mesh,
        in_specs=(
            P("seq", None),
            P("seq", None),
            P("seq"),
            P("seq", None),
            P("seq", None),
            P("seq", None),
            P("seq", None),
            P("seq", None),
            P(None, "seq"),
            P("seq"),
            P("seq"),
            P("seq", None),
            P("seq"),
            P("seq", None),
            P("seq", None),
            P("seq", None),
        ),
        out_specs=(
            P("seq", None),
            P("seq", None),
            P("seq"),
            P("seq", None),
            P("seq", None),
            P("seq", None),
            P("seq", None),
            P("seq", None),
            P(None, "seq"),
            P("seq"),
            P("seq"),
            P("seq", None),
            P("seq"),
            P("seq", None),
            P("seq", None),
            P("seq", None),
        ),
        check_vma=False,
    )
```
